256 devices in a mesh: blk: 128 (over y_hi, z, x, core), cat: 2 (over y_lo).
Axes of the slice: x: 4, y: 4 (y_hi: 2, y_lo: 2; y = y_hi * 2 + y_lo), z: 8, core: 2. Of those that a mesh axis runs over, the one named last changes fastest.
Arguments:
- item_content: bfloat16 [262144, 512], P('blk', 'cat'), may hold values from -6 to 6
- projection: bfloat16 [512, 256], replicated, may hold values from -0.06591797 to 0.06591797
- send_order: int32 [256, 1024], P(('blk', 'cat')), may hold values from 0 to 1023, each once within a row
- user_factors: float32 [131072, 256], P(('blk', 'cat')), may hold values from -1.5 to 1.5
- ratings: int32 [131072, 4, 1024], P(('blk', 'cat')), may hold values from 0 to 5, as said below
Outputs:
- users_out: float32 [131072, 256], P(('blk', 'cat'))
- items_out: float32 [262144, 256], P(('blk', 'cat'))
The draws below stay inside these ranges and needn't reach their ends.
Inputs may be any that keep to these rules, and one draw needn't show every extreme that they name: `send_order`: each row is a permutation of 0 .. 1023. `ratings`: 0 means no rating, 1 to 5 a rating.
All inputs are finite; a program needn't handle non-finite values.
Results may differ from the reference program's by a relative error of at most 0.0003.
Values may be sent and summed in bfloat16 or wider, within the bound.
No kernel may reach another device: no remote copies, remote signals or barrier semaphores. Data moves between devices by JAX's collectives and lax.ppermute only.
A program may use at most 64 MiB of HBM per device.

```python
import jax
import jax.numpy as jnp
from jax import lax

R = 256
C = 512
U_DEV = 512
ITEM_DEV = 1024
ROUNDS = 4
USERS = 131072
ITEMS = 262144
N_BLK = 128
N_CAT = 2
DEVICES = 256


def draw_ratings(key, part):
    shape = (USERS, ROUNDS, ITEM_DEV)
    levels = jax.random.randint(jax.random.fold_in(key, 11), shape, 1, 6)
    present = jax.random.randint(jax.random.fold_in(key, 12), shape, 0, 3)
    return jnp.where(present == 0, levels, 0).astype(jnp.int32)


def block_scale(rng, shape, cuts, smallest, largest):
    gain, own = 1.0, jax.random.fold_in(rng, 6)
    for axis_at, blocks in cuts:
        steps = jnp.exp(jax.random.uniform(jax.random.fold_in(own, axis_at), (blocks,), jnp.float32, smallest / len(cuts), largest / len(cuts)))
        gain = gain * jnp.repeat(steps, shape[axis_at] // blocks).reshape([-1 if axis == axis_at else 1 for axis in range(len(shape))])
    return gain


def noise(key, shape, width, bound, cuts=(), held_as=jnp.bfloat16):
    gain = block_scale(key, shape, cuts, -0.22, 0.18) if cuts else 1.0
    drawn = jax.random.normal(key, shape, jnp.float32) * width * gain
    return jnp.minimum(jnp.maximum(drawn, -bound), bound).astype(held_as)


def setup_inputs(seed: int = 0) -> dict:
    keys = jax.random.split(jax.random.key(seed), 6)
    item_content = noise(keys[0], (ITEMS, C), 1.0, 6.0, ((0, 128), (1, 2)))
    projection = noise(keys[1], (C, R), 0.011, 0.06591797)
    send_order = jax.vmap(lambda own: jax.random.permutation(own, ITEM_DEV))(jax.random.split(keys[2], DEVICES)).reshape((DEVICES, ITEM_DEV)).astype(jnp.int32)
    user_factors = noise(keys[3], (USERS, R), 0.25, 1.5, ((0, 256),), jnp.float32)
    ratings = draw_ratings(jax.random.fold_in(keys[5], 71), 0)
    return dict(item_content=item_content, projection=projection, send_order=send_order, user_factors=user_factors, ratings=ratings)


learn_rate = 0.004
shrink = 0.05


def reference(item_content, projection, send_order, user_factors, ratings):
    projected = jnp.dot(item_content, projection, preferred_element_type=jnp.float32)
    blocks = projected.reshape(N_BLK, N_CAT, ITEM_DEV, R)
    orders = send_order.reshape(N_BLK, N_CAT, ITEM_DEV)
    dealt = jnp.take_along_axis(blocks, orders[..., None], axis=2)
    share = ITEM_DEV // N_BLK
    items = dealt.reshape(N_BLK, N_CAT, N_BLK, share, R).transpose(2, 1, 0, 3, 4).reshape(N_BLK, N_CAT, ITEM_DEV, R)
    users = user_factors.reshape(N_BLK, N_CAT, U_DEV, R)
    values_all = ratings.reshape(N_BLK, N_CAT, U_DEV, ROUNDS, ITEM_DEV)
    for round_index in range(ROUNDS):
        if round_index > 0:
            items = jnp.roll(items, 1, axis=0)
        values = values_all[:, :, :, round_index, :].astype(jnp.float32)
        masks = jnp.where(values > 0, jnp.float32(1.0), jnp.float32(0.0))
        guess = jnp.einsum("bcur,bcir->bcui", users, items, precision=lax.Precision.HIGHEST)
        errors = masks * (values - guess)
        user_grad = jnp.einsum("bcui,bcir->bcur", errors, items, precision=lax.Precision.HIGHEST)
        item_grad = jnp.einsum("bcui,bcur->bcir", errors, users, precision=lax.Precision.HIGHEST)
        users, items = (users + learn_rate * (user_grad - shrink * users),
                        items + learn_rate * (item_grad - shrink * items))
    return users.reshape(USERS, R), items.reshape(ITEMS, R)
```

```python
import functools

import jax
import jax.numpy as jnp
from jax import lax
from jax.experimental import pallas as pl
from jax.experimental.pallas import tpu as pltpu
from jax.sharding import PartitionSpec as P

ROUNDS = 4
learn_rate = 0.004
shrink = 0.05
KEEP = 1.0 - learn_rate * shrink
CONTENT_BOUND = 6.0
LOG_RANGE = 14.0
TOP = 32767.0
EVEN_PIECES = 2
ODD_PIECES = 2
EVEN_TAIL = 16
ODD_TAIL = 8
F32 = jnp.float32
BF16 = jnp.bfloat16
I32 = jnp.int32

VM = pl.BlockSpec(memory_space=pltpu.VMEM)
SM = pl.BlockSpec(memory_space=pltpu.SMEM)
ANY = pl.BlockSpec(memory_space=pl.ANY)


def params(limit=12):
    return pltpu.CompilerParams(vmem_limit_bytes=limit << 20)


def cost(flops, moved):
    return pl.CostEstimate(flops=flops, bytes_accessed=moved, transcendentals=0)


def split(x):
    hi = x.astype(BF16)
    return hi, (x - hi.astype(F32)).astype(BF16)


def mm(a, b, dims=((1,), (0,))):
    return lax.dot_general(a, b, (dims, ((), ())), preferred_element_type=F32)


def pack(a, b):
    return lax.shift_left(a, 16) | (b & 0xFFFF)


def unpack(w):
    return (
        lax.shift_right_arithmetic(w, 16).astype(F32),
        lax.shift_right_arithmetic(lax.shift_left(w, 16), 16).astype(F32),
    )


def rounded(x):
    return jnp.round(x).astype(I32)


def log_scale(bound):
    floor = bound * (2.0 ** -LOG_RANGE)
    return floor, TOP / (jnp.log2(1.0 + 2.0 ** LOG_RANGE) * 1.0001)


def log_code(x, bound):
    floor, scale = log_scale(bound)
    size = jnp.minimum(jnp.log2(1.0 + jnp.abs(x) / floor) * scale, TOP)
    return rounded(jnp.where(x < 0, -size, size))


def log_value(code, bound):
    floor, scale = log_scale(bound)
    size = (jnp.exp2(jnp.abs(code) * (1.0 / scale)) - 1.0) * floor
    return jnp.where(code < 0, -size, size)


def put_users(p, users, left, left_t):
    hi, lo = split(p)
    if users is not None:
        users[...] = p
    left[0] = hi
    left[1] = lo
    hi_t, lo_t = split(p.T)
    left_t[0] = hi_t
    left_t[1] = lo_t


def before_kernel(flags, order, content, weights, users, deal, partial, meta, left, left_t, rows, sem):
    n = order.shape[1]
    part = flags[0]
    copy = pltpu.make_async_copy(content.at[pl.ds(pl.multiple_of(part * n, n), n), :], rows, sem)
    copy.start()
    column_sums = jnp.sum(jnp.abs(weights[...].astype(F32)), axis=0, keepdims=True)
    bound = jnp.maximum(jnp.max(column_sums, axis=1, keepdims=True) * (CONTENT_BOUND * 1.001), 1e-30)
    meta[...] = jnp.broadcast_to(bound, meta.shape)
    lanes = lax.broadcasted_iota(I32, (128, n), 1)
    for at in range(0, n, 128):
        wide = jnp.broadcast_to(order[:, at:at + 128], (128, 128)).T
        picked = jnp.concatenate([wide] * (n // 128), axis=1) == lanes
        deal[at:at + 128, :] = jnp.where(picked, 1.0, 0.0).astype(BF16)
    put_users(users[...], None, left, left_t)
    copy.wait()
    depth = content.shape[1]
    mine = weights[pl.ds(pl.multiple_of(part * depth, depth), depth), :]
    partial[...] = mm(mm(deal[...], rows[...]).astype(BF16), mine)


def project_kernel(flags, deal, first, second, weights, partial, meta, out):
    other = 1 - flags[0]
    depth = first.shape[1]
    half = first.shape[0]
    theirs = weights[pl.ds(pl.multiple_of(other * depth, depth), depth), :]
    rows = mm(deal[:, :half], first[...]) + mm(deal[:, half:], second[...])
    x = partial[...] + mm(rows.astype(BF16), theirs)
    code = log_code(x, meta[0:1, 0:1])
    mid = x.shape[1] // 2
    out[...] = pack(code[:, :mid], code[:, mid:])


def ratings_kernel(ratings, *outs):
    for t, out in enumerate(outs):
        out[...] = ratings[:, t, :].astype(F32).astype(BF16)


def encode(x):
    top = jnp.maximum(jnp.max(jnp.abs(x), axis=0, keepdims=True), 1e-30)
    level = jnp.ceil(jnp.log2(top) * 65536.0).astype(I32) + 4
    scale = TOP / jnp.exp2(level.astype(F32) * (1.0 / 65536.0))
    code = rounded(jnp.clip(x * scale, -TOP, TOP))
    mid = x.shape[0] // 2
    return pack(code[:mid], code[mid:]), level


def decode(w, rank):
    rows = rank // 2
    a, b = unpack(w[:rows, :])
    scale = jnp.exp2(w[rows:rows + 1, :].astype(F32) * (1.0 / 65536.0)) * (1.0 / TOP)
    return jnp.concatenate([a, b], axis=0) * scale


def errors_and_items(q, cols, left, left_t, values, err, right):
    q_hi, q_lo = split(q)
    if right is not None:
        right[0, :, cols] = q_hi
        right[1, :, cols] = q_lo
    guess = mm(left[0], q_hi) + mm(left[0], q_lo) + mm(left[1], q_hi)
    v = values[:, cols].astype(F32)
    e_hi, e_lo = split(jnp.where(v > 0, v - guess, 0.0))
    err[0, :, cols] = e_hi
    err[1, :, cols] = e_lo
    grad = mm(left_t[0], e_hi) + mm(left_t[0], e_lo) + mm(left_t[1], e_hi)
    return KEEP * q + learn_rate * grad


def first_items(dealt, meta, cols):
    w = dealt[cols, :].T
    a, b = unpack(w)
    return log_value(jnp.concatenate([a, b], axis=0), meta[0:1, 0:1])


CHUNK = 256


def piece(refs, at):
    wide = refs[0].shape[1]
    return refs[at // wide], slice(at % wide, at % wide + CHUNK)


def push_kernel(turn, first, pieces, *refs):
    flags, left, left_t, values = refs[:4]
    refs = refs[4:]
    if first:
        dealt, meta = refs[:2]
        refs = refs[2:]
    else:
        got = refs[:-2 - pieces]
        refs = refs[-2 - pieces:]
    err, right = refs[:2]
    outs = refs[2:]
    n = values.shape[1]

    @pl.when(flags[1] == turn)
    def _():
        for at in range(0, n, CHUNK):
            cols = slice(at, at + CHUNK)
            if first:
                q = first_items(dealt, meta, cols)
            else:
                ref, here = piece(got, at)
                q = decode(ref[:, here], right.shape[1])
            words, level = encode(errors_and_items(q, cols, left, left_t, values, err, right))
            rows = words.shape[0]
            ref, here = piece(outs, at)
            ref[:rows, here] = words
            ref[rows:, here] = jnp.broadcast_to(level, (ref.shape[0] - rows, CHUNK))


def user_step(users, err, right):
    dims = ((1,), (1,))
    grad = mm(err[0], right[0], dims) + mm(err[0], right[1], dims) + mm(err[1], right[0], dims)
    return KEEP * users[...] + learn_rate * grad


def pull_kernel(flags, users, err_odd, right_odd, err_even, right_even, new_users, left, left_t):
    for turn, err, right in ((1, err_odd, right_odd), (0, err_even, right_even)):

        @pl.when(flags[1] == turn)
        def _():
            put_users(user_step(users, err, right), new_users, left, left_t)


def last_kernel(flags, left, left_t, values, users, *refs):
    even = refs[:EVEN_PIECES]
    odd = refs[EVEN_PIECES:EVEN_PIECES + ODD_PIECES]
    users_out, items_out, err, right = refs[EVEN_PIECES + ODD_PIECES:]
    is_odd = flags[1] == 1
    for at in range(0, values.shape[1], CHUNK):
        cols = slice(at, at + CHUNK)
        (a, at_a), (b, at_b) = piece(odd, at), piece(even, at)
        live = right.shape[1] // 2 + 8
        q = decode(jnp.where(is_odd, a[:live, at_a], b[:live, at_b]), right.shape[1])
        items_out[cols, :] = errors_and_items(q, cols, left, left_t, values, err, right).T
    users_out[...] = user_step(users, err, right)


def struct(shape, dtype):
    return jax.ShapeDtypeStruct(shape, dtype)


def body(n_blk, item_content, projection, send_order, user_factors, ratings):
    n_users, rank = user_factors.shape
    n_items = send_order.shape[1]
    depth = item_content.shape[1]
    share = n_items // n_blk
    wide = n_items // 2
    part = lax.axis_index("cat")
    place = lax.axis_index("blk")
    flags = jnp.stack([part, lax.rem(place, 2)]).astype(I32)
    swap = [(0, 1), (1, 0)]
    away = lax.dynamic_slice_in_dim(item_content, (1 - part) * n_items, n_items, axis=0)
    came = [lax.ppermute(away[i * wide:(i + 1) * wide], "cat", swap) for i in range(2)]
    split_shapes = [struct((2, n_users, rank), BF16), struct((2, rank, n_users), BF16)]
    deal, partial, meta, left, left_t = pl.pallas_call(
        before_kernel,
        out_shape=[
            struct((n_items, n_items), BF16),
            struct((n_items, rank), F32),
            struct((8, 128), F32),
        ] + split_shapes,
        in_specs=[SM, VM, ANY, VM, VM],
        out_specs=[VM] * 5,
        scratch_shapes=[pltpu.VMEM((n_items, depth), BF16), pltpu.SemaphoreType.DMA],
        compiler_params=params(),
        cost_estimate=cost(2 * n_items * n_items * depth, 6 << 20),
        name="before",
    )(flags, send_order, item_content, projection, user_factors)
    coded = pl.pallas_call(
        project_kernel,
        out_shape=struct((n_items, rank // 2), I32),
        in_specs=[SM] + [VM] * 6,
        out_specs=VM,
        compiler_params=params(),
        cost_estimate=cost(2 * n_items * n_items * depth, 4 << 20),
        name="project",
    )(flags, deal, came[0], came[1], projection, partial, meta)
    dealt = lax.all_to_all(
        coded.reshape(n_blk, share, rank // 2), "blk", split_axis=0, concat_axis=0, tiled=True
    ).reshape(n_items, rank // 2)
    ratings, coded = lax.optimization_barrier((ratings, coded))
    rows = 64
    values = pl.pallas_call(
        ratings_kernel,
        out_shape=[struct((n_users, n_items), BF16)] * ROUNDS,
        grid=(n_users // rows,),
        in_specs=[pl.BlockSpec((rows, ROUNDS, n_items), lambda i: (i, 0, 0))],
        out_specs=[pl.BlockSpec((rows, n_items), lambda i: (i, 0))] * ROUNDS,
        compiler_params=params(32),
        cost_estimate=cost(1 << 20, 12 << 20),
        name="ratings",
    )(ratings)

    state_shapes = [struct((2, n_users, n_items), BF16), struct((2, rank, n_items), BF16)]
    round_cost = cost(2 * n_users * n_items * rank * 6, 6 << 20)
    to_even = [(i, (i + 1) % n_blk) for i in range(1, n_blk, 2)]
    to_odd = [(i, i + 1) for i in range(0, n_blk, 2)]

    def push(turn, source, pieces, tail, flags=flags):
        sent_shapes = [struct((rank // 2 + tail, n_items // pieces), I32)] * pieces
        first = len(source) == 2 and source[0].shape[0] == n_items
        ins = [flags, left, left_t, values[t], *source]
        got = pl.pallas_call(
            functools.partial(push_kernel, turn, first, pieces),
            out_shape=state_shapes + sent_shapes,
            in_specs=[SM] + [VM] * (len(ins) - 1),
            out_specs=[VM] * (2 + pieces),
            compiler_params=params(),
            cost_estimate=cost(1 << 10, 1 << 10),
            name="push",
        )(*ins)
        return got[:2], got[2:]

    users = user_factors
    for_odd = for_even = [dealt, meta]
    for t in range(ROUNDS - 1):
        state_odd, sent = push(1, for_odd, EVEN_PIECES, EVEN_TAIL)
        next_even = [lax.ppermute(x, "blk", to_even) for x in sent]
        later, _ = lax.optimization_barrier((flags, sent[0]))
        state_even, sent = push(0, for_even, ODD_PIECES, ODD_TAIL, later)
        next_odd = [lax.ppermute(x, "blk", to_odd) for x in sent]
        users, left, left_t = pl.pallas_call(
            pull_kernel,
            out_shape=[struct((n_users, rank), F32)] + split_shapes,
            in_specs=[SM] + [VM] * 5,
            out_specs=[VM] * 3,
            compiler_params=params(),
            cost_estimate=cost(1 << 10, 1 << 10),
            name="pull",
        )(flags, users, *state_odd, *state_even)
        for_even, for_odd = next_even, next_odd
    return tuple(pl.pallas_call(
        last_kernel,
        out_shape=[struct((n_users, rank), F32), struct((n_items, rank), F32)],
        in_specs=[SM] + [VM] * (4 + EVEN_PIECES + ODD_PIECES),
        out_specs=[VM] * 2,
        scratch_shapes=[
            pltpu.VMEM((2, n_users, n_items), BF16),
            pltpu.VMEM((2, rank, n_items), BF16),
        ],
        compiler_params=params(),
        cost_estimate=round_cost,
        name="last",
    )(flags, left, left_t, values[ROUNDS - 1], users, *for_even, *for_odd))


def solution(mesh):
    placed = (
        P("blk", "cat"),
        P(),
        P(("blk", "cat"), None),
        P(("blk", "cat"), None),
        P(("blk", "cat"), None, None),
    )
    return jax.shard_map(
        functools.partial(body, mesh.shape["blk"]),
        mesh=mesh,
        in_specs=placed,
        out_specs=(P(("blk", "cat"), None), P(("blk", "cat"), None)),
        check_vma=False,
    )
```

```python
import functools

import jax
import jax.numpy as jnp
from jax import lax
from jax.experimental import pallas as pl
from jax.experimental.pallas import tpu as pltpu
from jax.sharding import PartitionSpec as P

ROUNDS = 4
learn_rate = 0.004
shrink = 0.05
KEEP = 1.0 - learn_rate * shrink
CONTENT_BOUND = 6.0
LOG_RANGE = 14.0
TOP = 32767.0
EVEN_PIECES = 2
ODD_PIECES = 2
EVEN_TAIL = 16
ODD_TAIL = 8
F32 = jnp.float32
BF16 = jnp.bfloat16
I32 = jnp.int32

VM = pl.BlockSpec(memory_space=pltpu.VMEM)
SM = pl.BlockSpec(memory_space=pltpu.SMEM)
HBM = pl.BlockSpec(memory_space=pltpu.HBM)


def params(limit=12):
    return pltpu.CompilerParams(vmem_limit_bytes=limit << 20)


def cost(flops, moved):
    return pl.CostEstimate(flops=flops, bytes_accessed=moved, transcendentals=0)


def split(x):
    hi = x.astype(BF16)
    return hi, (x - hi.astype(F32)).astype(BF16)


def mm(a, b, dims=((1,), (0,))):
    return lax.dot_general(a, b, (dims, ((), ())), preferred_element_type=F32)


def pack(a, b):
    return lax.shift_left(a, 16) | (b & 0xFFFF)


def unpack(w):
    return (
        lax.shift_right_arithmetic(w, 16).astype(F32),
        lax.shift_right_arithmetic(lax.shift_left(w, 16), 16).astype(F32),
    )


def rounded(x):
    return jnp.round(x).astype(I32)


def log_scale(bound):
    floor = bound * (2.0 ** -LOG_RANGE)
    return floor, TOP / (jnp.log2(1.0 + 2.0 ** LOG_RANGE) * 1.0001)


def log_code(x, bound):
    floor, scale = log_scale(bound)
    size = jnp.minimum(jnp.log2(1.0 + jnp.abs(x) / floor) * scale, TOP)
    return rounded(jnp.where(x < 0, -size, size))


def log_value(code, bound):
    floor, scale = log_scale(bound)
    size = (jnp.exp2(jnp.abs(code) * (1.0 / scale)) - 1.0) * floor
    return jnp.where(code < 0, -size, size)


def put_users(p, users, left, left_t):
    hi, lo = split(p)
    if users is not None:
        users[...] = p
    left[0] = hi
    left[1] = lo
    hi_t, lo_t = split(p.T)
    left_t[0] = hi_t
    left_t[1] = lo_t


def before_kernel(flags, order, content, weights, users, deal, partial, meta, left, left_t, rows, held, sems):
    n = order.shape[1]
    part = flags[0]
    copy = pltpu.make_async_copy(content.at[pl.ds(pl.multiple_of(part * n, n), n), :], rows, sems.at[0])
    copy.start()
    users_copy = pltpu.make_async_copy(users, held, sems.at[1])
    users_copy.start()
    column_sums = jnp.sum(jnp.abs(weights[...].astype(F32)), axis=0, keepdims=True)
    bound = jnp.maximum(jnp.max(column_sums, axis=1, keepdims=True) * (CONTENT_BOUND * 1.001), 1e-30)
    meta[...] = jnp.broadcast_to(bound, meta.shape)
    lanes = lax.broadcasted_iota(I32, (128, n), 1)
    for at in range(0, n, 128):
        wide = jnp.broadcast_to(order[:, at:at + 128], (128, 128)).T
        picked = jnp.concatenate([wide] * (n // 128), axis=1) == lanes
        deal[at:at + 128, :] = jnp.where(picked, 1.0, 0.0).astype(BF16)
    users_copy.wait()
    put_users(held[...], None, left, left_t)
    copy.wait()
    depth = content.shape[1]
    mine = weights[pl.ds(pl.multiple_of(part * depth, depth), depth), :]
    partial[...] = mm(mm(deal[...], rows[...]).astype(BF16), mine)


def project_kernel(flags, deal, first, second, weights, partial, meta, out):
    other = 1 - flags[0]
    depth = first.shape[1]
    half = first.shape[0]
    theirs = weights[pl.ds(pl.multiple_of(other * depth, depth), depth), :]
    rows = mm(deal[:, :half], first[...]) + mm(deal[:, half:], second[...])
    x = partial[...] + mm(rows.astype(BF16), theirs)
    code = log_code(x, meta[0:1, 0:1])
    mid = x.shape[1] // 2
    out[...] = pack(code[:, :mid], code[:, mid:])


def ratings_kernel(ratings, out):
    n, wide = out.shape
    groups = wide // 128
    for g in range(groups):
        word = None
        for t in reversed(range(ROUNDS)):
            rows = ratings[pl.ds(g * ROUNDS + t, n, stride=groups * ROUNDS), :]
            word = rows if word is None else lax.shift_left(word, 3) | rows
        out[:, g * 128:(g + 1) * 128] = word.astype(jnp.int16)


def encode(x):
    top = jnp.maximum(jnp.max(jnp.abs(x), axis=0, keepdims=True), 1e-30)
    level = jnp.ceil(jnp.log2(top) * 65536.0).astype(I32) + 4
    scale = TOP / jnp.exp2(level.astype(F32) * (1.0 / 65536.0))
    code = rounded(jnp.clip(x * scale, -TOP, TOP))
    mid = x.shape[0] // 2
    return pack(code[:mid], code[mid:]), level


def decode(w, rank):
    rows = rank // 2
    a, b = unpack(w[:rows, :])
    scale = jnp.exp2(w[rows:rows + 1, :].astype(F32) * (1.0 / 65536.0)) * (1.0 / TOP)
    return jnp.concatenate([a, b], axis=0) * scale


def errors_and_items(q, cols, left, left_t, values, t, err, right):
    q_hi, q_lo = split(q)
    if right is not None:
        right[0, :, cols] = q_hi
        right[1, :, cols] = q_lo
    guess = mm(left[0], q_hi) + mm(left[0], q_lo) + mm(left[1], q_hi)
    v = (lax.shift_right_logical(values[:, cols].astype(I32), 3 * t) & 7).astype(F32)
    e_hi, e_lo = split(jnp.where(v > 0, v - guess, 0.0))
    err[0, :, cols] = e_hi
    err[1, :, cols] = e_lo
    grad = mm(left_t[0], e_hi) + mm(left_t[0], e_lo) + mm(left_t[1], e_hi)
    return KEEP * q + learn_rate * grad


def first_items(dealt, meta, cols):
    w = dealt[cols, :].T
    a, b = unpack(w)
    return log_value(jnp.concatenate([a, b], axis=0), meta[0:1, 0:1])


CHUNK = 256


def piece(refs, at):
    wide = refs[0].shape[1]
    return refs[at // wide], slice(at % wide, at % wide + CHUNK)


def push_kernel(turn, t, pieces, *refs):
    first = t == 0
    flags, left, left_t, values = refs[:4]
    refs = refs[4:]
    if first:
        dealt, meta = refs[:2]
        refs = refs[2:]
    else:
        got = refs[:-2 - pieces]
        refs = refs[-2 - pieces:]
    err, right = refs[:2]
    outs = refs[2:]
    n = values.shape[1]

    @pl.when(flags[1] == turn)
    def _():
        for at in range(0, n, CHUNK):
            cols = slice(at, at + CHUNK)
            if first:
                q = first_items(dealt, meta, cols)
            else:
                ref, here = piece(got, at)
                q = decode(ref[:, here], right.shape[1])
            words, level = encode(errors_and_items(q, cols, left, left_t, values, t, err, right))
            rows = words.shape[0]
            ref, here = piece(outs, at)
            ref[:rows, here] = words
            ref[rows:, here] = jnp.broadcast_to(level, (ref.shape[0] - rows, CHUNK))


def user_step(users, err, right):
    dims = ((1,), (1,))
    grad = mm(err[0], right[0], dims) + mm(err[0], right[1], dims) + mm(err[1], right[0], dims)
    return KEEP * users[...] + learn_rate * grad


def pull_kernel(flags, users, err_odd, right_odd, err_even, right_even, new_users, left, left_t):
    for turn, err, right in ((1, err_odd, right_odd), (0, err_even, right_even)):

        @pl.when(flags[1] == turn)
        def _():
            put_users(user_step(users, err, right), new_users, left, left_t)


def last_kernel(flags, left, left_t, values, users, *refs):
    even = refs[:EVEN_PIECES]
    odd = refs[EVEN_PIECES:EVEN_PIECES + ODD_PIECES]
    users_out, items_out, err, right = refs[EVEN_PIECES + ODD_PIECES:]
    is_odd = flags[1] == 1
    t = ROUNDS - 1
    for at in range(0, values.shape[1], CHUNK):
        cols = slice(at, at + CHUNK)
        (a, at_a), (b, at_b) = piece(odd, at), piece(even, at)
        live = right.shape[1] // 2 + 8
        q = decode(jnp.where(is_odd, a[:live, at_a], b[:live, at_b]), right.shape[1])
        items_out[cols, :] = errors_and_items(q, cols, left, left_t, values, t, err, right).T
    users_out[...] = user_step(users, err, right)


def struct(shape, dtype):
    return jax.ShapeDtypeStruct(shape, dtype)


def body(n_blk, item_content, projection, send_order, user_factors, ratings):
    n_users, rank = user_factors.shape
    n_items = send_order.shape[1]
    depth = item_content.shape[1]
    share = n_items // n_blk
    wide = n_items // 2
    part = lax.axis_index("cat")
    place = lax.axis_index("blk")
    flags = jnp.stack([part, lax.rem(place, 2)]).astype(I32)
    swap = [(0, 1), (1, 0)]
    away = lax.dynamic_slice_in_dim(item_content, (1 - part) * n_items, n_items, axis=0)
    came = [lax.ppermute(away[i * wide:(i + 1) * wide], "cat", swap) for i in range(2)]
    split_shapes = [struct((2, n_users, rank), BF16), struct((2, rank, n_users), BF16)]
    deal, partial, meta, left, left_t = pl.pallas_call(
        before_kernel,
        out_shape=[
            struct((n_items, n_items), BF16),
            struct((n_items, rank), F32),
            struct((8, 128), F32),
        ] + split_shapes,
        in_specs=[SM, VM, HBM, VM, HBM],
        out_specs=[VM] * 5,
        scratch_shapes=[
            pltpu.VMEM((n_items, depth), BF16),
            pltpu.VMEM((n_users, rank), F32),
            pltpu.SemaphoreType.DMA((2,)),
        ],
        compiler_params=params(),
        cost_estimate=cost(2 * n_items * n_items * depth, 6 << 20),
        name="before",
    )(flags, send_order, item_content, projection, user_factors)
    coded = pl.pallas_call(
        project_kernel,
        out_shape=struct((n_items, rank // 2), I32),
        in_specs=[SM] + [VM] * 6,
        out_specs=VM,
        compiler_params=params(),
        cost_estimate=cost(2 * n_items * n_items * depth, 4 << 20),
        name="project",
    )(flags, deal, came[0], came[1], projection, partial, meta)
    dealt = lax.all_to_all(
        coded.reshape(n_blk, share, rank // 2), "blk", split_axis=0, concat_axis=0, tiled=True
    ).reshape(n_items, rank // 2)
    ratings, coded = lax.optimization_barrier((ratings, coded))
    rows = 64
    groups = n_items // 128
    ratings = ratings.reshape(n_users, ROUNDS, groups, 128).transpose(0, 2, 1, 3)
    ratings = ratings.reshape(n_users * groups * ROUNDS, 128)
    values = pl.pallas_call(
        ratings_kernel,
        out_shape=struct((n_users, n_items), jnp.int16),
        grid=(n_users // rows,),
        in_specs=[pl.BlockSpec((rows * groups * ROUNDS, 128), lambda i: (i, 0))],
        out_specs=pl.BlockSpec((rows, n_items), lambda i: (i, 0)),
        compiler_params=params(52),
        cost_estimate=cost(1 << 20, 12 << 20),
        name="ratings",
    )(ratings)

    state_shapes = [struct((2, n_users, n_items), BF16), struct((2, rank, n_items), BF16)]
    round_cost = cost(2 * n_users * n_items * rank * 6, 6 << 20)
    to_even = [(i, (i + 1) % n_blk) for i in range(1, n_blk, 2)]
    to_odd = [(i, i ^ 1) for i in range(n_blk)]

    def push(turn, source, pieces, tail, flags=flags):
        sent_shapes = [struct((rank // 2 + tail, n_items // pieces), I32)] * pieces
        ins = [flags, left, left_t, values, *source]
        got = pl.pallas_call(
            functools.partial(push_kernel, turn, t, pieces),
            out_shape=state_shapes + sent_shapes,
            in_specs=[SM] + [VM] * (len(ins) - 1),
            out_specs=[VM] * (2 + pieces),
            compiler_params=params(),
            cost_estimate=cost(1 << 10, 1 << 10),
            name="push",
        )(*ins)
        return got[:2], got[2:]

    users = user_factors
    for_odd = for_even = [dealt, meta]
    for t in range(ROUNDS - 1):
        state_odd, sent = push(1, for_odd, EVEN_PIECES, EVEN_TAIL)
        next_even = [lax.ppermute(x, "blk", to_even) for x in sent]
        later, _ = lax.optimization_barrier((flags, sent[0]))
        state_even, sent = push(0, for_even, ODD_PIECES, ODD_TAIL, later)
        next_odd = [lax.ppermute(x, "blk", to_odd) for x in sent]
        users, left, left_t = pl.pallas_call(
            pull_kernel,
            out_shape=[struct((n_users, rank), F32)] + split_shapes,
            in_specs=[SM] + [VM] * 5,
            out_specs=[VM] * 3,
            compiler_params=params(),
            cost_estimate=cost(1 << 10, 1 << 10),
            name="pull",
        )(flags, users, *state_odd, *state_even)
        for_even, for_odd = next_even, next_odd
    return tuple(pl.pallas_call(
        last_kernel,
        out_shape=[struct((n_users, rank), F32), struct((n_items, rank), F32)],
        in_specs=[SM] + [VM] * (4 + EVEN_PIECES + ODD_PIECES),
        out_specs=[VM] * 2,
        scratch_shapes=[
            pltpu.VMEM((2, n_users, n_items), BF16),
            pltpu.VMEM((2, rank, n_items), BF16),
        ],
        compiler_params=params(),
        cost_estimate=round_cost,
        name="last",
    )(flags, left, left_t, values, users, *for_even, *for_odd))


def solution(mesh):
    placed = (
        P("blk", "cat"),
        P(),
        P(("blk", "cat"), None),
        P(("blk", "cat"), None),
        P(("blk", "cat"), None, None),
    )
    return jax.shard_map(
        functools.partial(body, mesh.shape["blk"]),
        mesh=mesh,
        in_specs=placed,
        out_specs=(P(("blk", "cat"), None), P(("blk", "cat"), None)),
        check_vma=False,
    )
```

```python
import functools

import jax
import jax.numpy as jnp
from jax import lax
from jax.experimental import pallas as pl
from jax.experimental.pallas import tpu as pltpu
from jax.sharding import PartitionSpec as P

ROUNDS = 4
learn_rate = 0.004
shrink = 0.05
KEEP = 1.0 - learn_rate * shrink
CONTENT_BOUND = 6.0
LOG_RANGE = 14.0
TOP = 32767.0
EVEN_PIECES = 2
ODD_PIECES = 2
EVEN_TAIL = 16
ODD_TAIL = 8
F32 = jnp.float32
BF16 = jnp.bfloat16
I32 = jnp.int32

VM = pl.BlockSpec(memory_space=pltpu.VMEM)
HBM = pl.BlockSpec(memory_space=pltpu.HBM)


def params(limit=12):
    return pltpu.CompilerParams(vmem_limit_bytes=limit << 20)


def cost(flops, moved):
    return pl.CostEstimate(flops=flops, bytes_accessed=moved, transcendentals=0)


def split(x):
    hi = x.astype(BF16)
    return hi, (x - hi.astype(F32)).astype(BF16)


def mm(a, b, dims=((1,), (0,))):
    return lax.dot_general(a, b, (dims, ((), ())), preferred_element_type=F32)


def pack(a, b):
    return lax.shift_left(a, 16) | (b & 0xFFFF)


def unpack(w):
    return (
        lax.shift_right_arithmetic(w, 16).astype(F32),
        lax.shift_right_arithmetic(lax.shift_left(w, 16), 16).astype(F32),
    )


def rounded(x):
    return jnp.round(x).astype(I32)


def log_scale(bound):
    floor = bound * (2.0 ** -LOG_RANGE)
    return floor, TOP / (jnp.log2(1.0 + 2.0 ** LOG_RANGE) * 1.0001)


def log_code(x, bound):
    floor, scale = log_scale(bound)
    size = jnp.minimum(jnp.log2(1.0 + jnp.abs(x) / floor) * scale, TOP)
    return rounded(jnp.where(x < 0, -size, size))


def log_value(code, bound):
    floor, scale = log_scale(bound)
    size = (jnp.exp2(jnp.abs(code) * (1.0 / scale)) - 1.0) * floor
    return jnp.where(code < 0, -size, size)


def put_users(p, users, left, left_t):
    hi, lo = split(p)
    if users is not None:
        users[...] = p
    left[0] = hi
    left[1] = lo
    hi_t, lo_t = split(p.T)
    left_t[0] = hi_t
    left_t[1] = lo_t


def before_kernel(order, content, weights, users, deal, partial, meta, left, left_t, rows, held, sems):
    n = order.shape[1]
    part = lax.axis_index("cat")
    copy = pltpu.make_async_copy(content.at[pl.ds(pl.multiple_of(part * n, n), n), :], rows, sems.at[0])
    copy.start()
    users_copy = pltpu.make_async_copy(users, held, sems.at[1])
    users_copy.start()
    column_sums = jnp.sum(jnp.abs(weights[...].astype(F32)), axis=0, keepdims=True)
    bound = jnp.maximum(jnp.max(column_sums, axis=1, keepdims=True) * (CONTENT_BOUND * 1.001), 1e-30)
    meta[...] = jnp.broadcast_to(bound, meta.shape)
    lanes = lax.broadcasted_iota(I32, (128, n), 1)
    for at in range(0, n, 128):
        wide = jnp.broadcast_to(order[:, at:at + 128], (128, 128)).T
        picked = jnp.concatenate([wide] * (n // 128), axis=1) == lanes
        deal[at:at + 128, :] = jnp.where(picked, 1.0, 0.0).astype(BF16)
    users_copy.wait()
    put_users(held[...], None, left, left_t)
    copy.wait()
    depth = content.shape[1]
    mine = weights[pl.ds(pl.multiple_of(part * depth, depth), depth), :]
    partial[...] = mm(mm(deal[...], rows[...]).astype(BF16), mine)


def project_kernel(deal, first, second, weights, partial, meta, out):
    other = 1 - lax.axis_index("cat")
    depth = first.shape[1]
    half = first.shape[0]
    theirs = weights[pl.ds(pl.multiple_of(other * depth, depth), depth), :]
    rows = mm(deal[:, :half], first[...]) + mm(deal[:, half:], second[...])
    x = partial[...] + mm(rows.astype(BF16), theirs)
    code = log_code(x, meta[0:1, 0:1])
    mid = x.shape[1] // 2
    out[...] = pack(code[:, :mid], code[:, mid:])


def ratings_kernel(ratings, out):
    n, wide = out.shape
    groups = wide // 128
    for g in range(groups):
        word = None
        for t in reversed(range(ROUNDS)):
            rows = ratings[pl.ds(g * ROUNDS + t, n, stride=groups * ROUNDS), :]
            word = rows if word is None else lax.shift_left(word, 3) | rows
        out[:, g * 128:(g + 1) * 128] = word.astype(jnp.int16)


def encode(x):
    top = jnp.maximum(jnp.max(jnp.abs(x), axis=0, keepdims=True), 1e-30)
    level = jnp.ceil(jnp.log2(top) * 65536.0).astype(I32) + 4
    scale = TOP / jnp.exp2(level.astype(F32) * (1.0 / 65536.0))
    code = rounded(jnp.clip(x * scale, -TOP, TOP))
    mid = x.shape[0] // 2
    return pack(code[:mid], code[mid:]), level


def decode(w, rank):
    rows = rank // 2
    a, b = unpack(w[:rows, :])
    scale = jnp.exp2(w[rows:rows + 1, :].astype(F32) * (1.0 / 65536.0)) * (1.0 / TOP)
    return jnp.concatenate([a, b], axis=0) * scale


def errors_and_items(q, cols, left, left_t, values, t, err, right):
    q_hi, q_lo = split(q)
    if right is not None:
        right[0, :, cols] = q_hi
        right[1, :, cols] = q_lo
    guess = mm(left[0], q_hi) + mm(left[0], q_lo) + mm(left[1], q_hi)
    v = (lax.shift_right_logical(values[:, cols].astype(I32), 3 * t) & 7).astype(F32)
    e_hi, e_lo = split(jnp.where(v > 0, v - guess, 0.0))
    err[0, :, cols] = e_hi
    err[1, :, cols] = e_lo
    grad = mm(left_t[0], e_hi) + mm(left_t[0], e_lo) + mm(left_t[1], e_hi)
    return KEEP * q + learn_rate * grad


def first_items(dealt, meta, cols):
    w = dealt[cols, :].T
    a, b = unpack(w)
    return log_value(jnp.concatenate([a, b], axis=0), meta[0:1, 0:1])


CHUNK = 256


def piece(refs, at):
    wide = refs[0].shape[1]
    return refs[at // wide], slice(at % wide, at % wide + CHUNK)


def my_turn(turn):
    return lax.rem(lax.axis_index("blk"), 2) == turn


def push_kernel(turn, t, pieces, *refs):
    first = t == 0
    left, left_t, values = refs[:3]
    refs = refs[3:]
    if first:
        dealt, meta = refs[:2]
        refs = refs[2:]
    else:
        got = refs[:-2 - pieces]
        refs = refs[-2 - pieces:]
    err, right = refs[:2]
    outs = refs[2:]
    n = values.shape[1]

    @pl.when(my_turn(turn))
    def _():
        for at in range(0, n, CHUNK):
            cols = slice(at, at + CHUNK)
            if first:
                q = first_items(dealt, meta, cols)
            else:
                ref, here = piece(got, at)
                q = decode(ref[:, here], right.shape[1])
            words, level = encode(errors_and_items(q, cols, left, left_t, values, t, err, right))
            rows = words.shape[0]
            ref, here = piece(outs, at)
            ref[:rows, here] = words
            ref[rows:, here] = jnp.broadcast_to(level, (ref.shape[0] - rows, CHUNK))


def user_step(users, err, right, rows=slice(None)):
    dims = ((1,), (1,))
    hi, lo = err[0, rows, :], err[1, rows, :]
    grad = mm(hi, right[0], dims) + mm(hi, right[1], dims) + mm(lo, right[0], dims)
    return KEEP * users[rows, :] + learn_rate * grad


def pull_kernel(turn, users, err, right, new_users, left, left_t):
    @pl.when(my_turn(turn))
    def _():
        put_users(user_step(users, err, right), new_users, left, left_t)


def last_kernel(pieces, *refs):
    odd, even = refs[:3], refs[3:6]
    values = refs[6]
    refs = refs[7:]
    to_odd, to_even = refs[:pieces[0]], refs[pieces[0]:sum(pieces)]
    users_out, items_out, err, right, users_held, items_held, sems = refs[sum(pieces):]
    n = values.shape[1]
    tall = users_held.shape[0] // 2

    for turn, (left, left_t, users), got in ((1, odd, to_odd), (0, even, to_even)):

        @pl.when(my_turn(turn))
        def _():
            copies = []
            for at in range(0, n, CHUNK):
                cols = slice(at, at + CHUNK)
                ref, here = piece(got, at)
                q = decode(ref[:, here], right.shape[1])
                new = errors_and_items(q, cols, left, left_t, values, ROUNDS - 1, err, right)
                items_held[cols, :] = new.T
                copies.append(pltpu.make_async_copy(items_held.at[cols, :], items_out.at[cols, :], sems.at[len(copies)]))
                copies[-1].start()
            for at in (0, tall):
                rows = slice(at, at + tall)
                users_held[rows, :] = user_step(users, err, right, rows)
                copies.append(pltpu.make_async_copy(users_held.at[rows, :], users_out.at[rows, :], sems.at[len(copies)]))
                copies[-1].start()
            for copy in copies:
                copy.wait()


def struct(shape, dtype):
    return jax.ShapeDtypeStruct(shape, dtype)


def body(n_blk, item_content, projection, send_order, user_factors, ratings):
    n_users, rank = user_factors.shape
    n_items = send_order.shape[1]
    depth = item_content.shape[1]
    share = n_items // n_blk
    wide = n_items // 2
    part = lax.axis_index("cat")
    swap = [(0, 1), (1, 0)]
    away = lax.dynamic_slice_in_dim(item_content, (1 - part) * n_items, n_items, axis=0)
    came = [lax.ppermute(away[i * wide:(i + 1) * wide], "cat", swap) for i in range(2)]
    rows = 64
    groups = n_items // 128
    ratings = ratings.reshape(n_users, ROUNDS, groups, 128).transpose(0, 2, 1, 3)
    ratings = ratings.reshape(n_users * groups * ROUNDS, 128)
    values = pl.pallas_call(
        ratings_kernel,
        out_shape=struct((n_users, n_items), jnp.int16),
        grid=(n_users // rows,),
        in_specs=[pl.BlockSpec((rows * groups * ROUNDS, 128), lambda i: (i, 0))],
        out_specs=pl.BlockSpec((rows, n_items), lambda i: (i, 0)),
        compiler_params=params(52),
        cost_estimate=cost(1 << 20, 12 << 20),
        name="ratings",
    )(ratings)
    send_order, values = lax.optimization_barrier((send_order, values))
    split_shapes = [struct((2, n_users, rank), BF16), struct((2, rank, n_users), BF16)]
    deal, partial, meta, left, left_t = pl.pallas_call(
        before_kernel,
        out_shape=[
            struct((n_items, n_items), BF16),
            struct((n_items, rank), F32),
            struct((8, 128), F32),
        ] + split_shapes,
        in_specs=[VM, HBM, VM, HBM],
        out_specs=[VM] * 5,
        scratch_shapes=[
            pltpu.VMEM((n_items, depth), BF16),
            pltpu.VMEM((n_users, rank), F32),
            pltpu.SemaphoreType.DMA((2,)),
        ],
        compiler_params=params(),
        cost_estimate=cost(2 * n_items * n_items * depth, 6 << 20),
        name="before",
    )(send_order, item_content, projection, user_factors)
    coded = pl.pallas_call(
        project_kernel,
        out_shape=struct((n_items, rank // 2), I32),
        in_specs=[VM] * 6,
        out_specs=VM,
        compiler_params=params(),
        cost_estimate=cost(2 * n_items * n_items * depth, 4 << 20),
        name="project",
    )(deal, came[0], came[1], projection, partial, meta)
    dealt = lax.all_to_all(
        coded.reshape(n_blk, share, rank // 2), "blk", split_axis=0, concat_axis=0, tiled=True
    ).reshape(n_items, rank // 2)

    state_shapes = [struct((2, n_users, n_items), BF16), struct((2, rank, n_items), BF16)]
    to_even = [(i, (i + 1) % n_blk) for i in range(1, n_blk, 2)]
    to_odd = [(i, i ^ 1) for i in range(n_blk)]
    light = cost(1 << 10, 1 << 10)

    def push(turn, t, left, left_t, source, pieces, tail):
        sent_shapes = [struct((rank // 2 + tail, n_items // pieces), I32)] * pieces
        got = pl.pallas_call(
            functools.partial(push_kernel, turn, t, pieces),
            out_shape=state_shapes + sent_shapes,
            in_specs=[VM] * (3 + len(source)),
            out_specs=[VM] * (2 + pieces),
            compiler_params=params(),
            cost_estimate=light,
            name="push",
        )(left, left_t, values, *source)
        return got[:2], got[2:]

    def pull(turn, users, state):
        return pl.pallas_call(
            functools.partial(pull_kernel, turn),
            out_shape=[struct((n_users, rank), F32)] + split_shapes,
            in_specs=[VM] * 3,
            out_specs=[VM] * 3,
            compiler_params=params(),
            cost_estimate=light,
            name="pull",
        )(users, *state)

    odd = even = (user_factors, left, left_t)
    for_odd = for_even = [dealt, meta]
    state_even = None
    for t in range(ROUNDS - 1):
        state_odd, sent = push(1, t, *odd[1:], for_odd, EVEN_PIECES, EVEN_TAIL)
        next_even = [lax.ppermute(x, "blk", to_even) for x in sent]
        if state_even is not None:
            users, _ = lax.optimization_barrier((even[0], sent[0]))
            even = pull(0, users, state_even)
        else:
            even = (even[0], lax.optimization_barrier((even[1], sent[0]))[0], even[2])
        state_even, sent = push(0, t, *even[1:], for_even, ODD_PIECES, ODD_TAIL)
        next_odd = [lax.ppermute(x, "blk", to_odd) for x in sent]
        odd = pull(1, odd[0], state_odd)
        for_even, for_odd = next_even, next_odd
    even = pull(0, even[0], state_even)
    return tuple(pl.pallas_call(
        functools.partial(last_kernel, (ODD_PIECES, EVEN_PIECES)),
        out_shape=[struct((n_users, rank), F32), struct((n_items, rank), F32)],
        in_specs=[VM] * (7 + EVEN_PIECES + ODD_PIECES),
        out_specs=[pl.BlockSpec(memory_space=pl.ANY)] * 2,
        scratch_shapes=[
            pltpu.VMEM((2, n_users, n_items), BF16),
            pltpu.VMEM((2, rank, n_items), BF16),
            pltpu.VMEM((n_users, rank), F32),
            pltpu.VMEM((n_items, rank), F32),
            pltpu.SemaphoreType.DMA((n_items // CHUNK + 2,)),
        ],
        compiler_params=params(16),
        cost_estimate=light,
        name="last",
    )(odd[1], odd[2], odd[0], even[1], even[2], even[0], values, *for_odd, *for_even))


def solution(mesh):
    placed = (
        P("blk", "cat"),
        P(),
        P(("blk", "cat"), None),
        P(("blk", "cat"), None),
        P(("blk", "cat"), None, None),
    )
    return jax.shard_map(
        functools.partial(body, mesh.shape["blk"]),
        mesh=mesh,
        in_specs=placed,
        out_specs=(P(("blk", "cat"), None), P(("blk", "cat"), None)),
        check_vma=False,
    )
```

```python
import functools

import jax
import jax.numpy as jnp
from jax import lax
from jax.experimental import pallas as pl
from jax.experimental.pallas import tpu as pltpu
from jax.sharding import PartitionSpec as P

ROUNDS = 4
learn_rate = 0.004
shrink = 0.05
KEEP = 1.0 - learn_rate * shrink
CONTENT_BOUND = 6.0
LOG_RANGE = 14.0
TOP = 32767.0
EVEN_TAILS = ((16, 16), (32, 24), (16, 16))
ODD_TAILS = ((8, 8), (8, 8), (8, 8))
F32 = jnp.float32
BF16 = jnp.bfloat16
I32 = jnp.int32

VM = pl.BlockSpec(memory_space=pltpu.VMEM)
HBM = pl.BlockSpec(memory_space=pltpu.HBM)


def params(limit=12):
    return pltpu.CompilerParams(vmem_limit_bytes=limit << 20)


def cost(flops, moved):
    return pl.CostEstimate(flops=flops, bytes_accessed=moved, transcendentals=0)


def split(x):
    hi = x.astype(BF16)
    return hi, (x - hi.astype(F32)).astype(BF16)


def mm(a, b, dims=((1,), (0,))):
    return lax.dot_general(a, b, (dims, ((), ())), preferred_element_type=F32)


def pack(a, b):
    return lax.shift_left(a, 16) | (b & 0xFFFF)


def unpack(w):
    return (
        lax.shift_right_arithmetic(w, 16).astype(F32),
        lax.shift_right_arithmetic(lax.shift_left(w, 16), 16).astype(F32),
    )


def rounded(x):
    return jnp.round(x).astype(I32)


def log_scale(bound):
    floor = bound * (2.0 ** -LOG_RANGE)
    return floor, TOP / (jnp.log2(1.0 + 2.0 ** LOG_RANGE) * 1.0001)


def log_code(x, bound):
    floor, scale = log_scale(bound)
    size = jnp.minimum(jnp.log2(1.0 + jnp.abs(x) / floor) * scale, TOP)
    return rounded(jnp.where(x < 0, -size, size))


def log_value(code, bound):
    floor, scale = log_scale(bound)
    size = (jnp.exp2(jnp.abs(code) * (1.0 / scale)) - 1.0) * floor
    return jnp.where(code < 0, -size, size)


def put_users(p, users, left, left_t):
    hi, lo = split(p)
    if users is not None:
        users[...] = p
    left[0] = hi
    left[1] = lo
    hi_t, lo_t = split(p.T)
    left_t[0] = hi_t
    left_t[1] = lo_t


def before_kernel(order, content, weights, users, deal, partial, meta, left, left_t, rows, held, sems):
    n = order.shape[1]
    part = lax.axis_index("cat")
    copy = pltpu.make_async_copy(content.at[pl.ds(pl.multiple_of(part * n, n), n), :], rows, sems.at[0])
    copy.start()
    users_copy = pltpu.make_async_copy(users, held, sems.at[1])
    users_copy.start()
    column_sums = jnp.sum(jnp.abs(weights[...].astype(F32)), axis=0, keepdims=True)
    bound = jnp.maximum(jnp.max(column_sums, axis=1, keepdims=True) * (CONTENT_BOUND * 1.001), 1e-30)
    meta[...] = jnp.broadcast_to(bound, meta.shape)
    lanes = lax.broadcasted_iota(I32, (128, n), 1)
    for at in range(0, n, 128):
        wide = jnp.broadcast_to(order[:, at:at + 128], (128, 128)).T
        picked = jnp.concatenate([wide] * (n // 128), axis=1) == lanes
        deal[at:at + 128, :] = jnp.where(picked, 1.0, 0.0).astype(BF16)
    users_copy.wait()
    put_users(held[...], None, left, left_t)
    copy.wait()
    depth = content.shape[1]
    mine = weights[pl.ds(pl.multiple_of(part * depth, depth), depth), :]
    partial[...] = mm(mm(deal[...], rows[...]).astype(BF16), mine)


def project_kernel(deal, first, second, weights, partial, meta, out):
    other = 1 - lax.axis_index("cat")
    depth = first.shape[1]
    half = first.shape[0]
    theirs = weights[pl.ds(pl.multiple_of(other * depth, depth), depth), :]
    rows = mm(deal[:, :half], first[...]) + mm(deal[:, half:], second[...])
    x = partial[...] + mm(rows.astype(BF16), theirs)
    code = log_code(x, meta[0:1, 0:1])
    mid = x.shape[1] // 2
    out[...] = pack(code[:, :mid], code[:, mid:])


def ratings_kernel(ratings, out):
    n, wide = out.shape
    groups = wide // 128
    for g in range(groups):
        word = None
        for t in reversed(range(ROUNDS)):
            rows = ratings[pl.ds(g * ROUNDS + t, n, stride=groups * ROUNDS), :]
            word = rows if word is None else lax.shift_left(word, 3) | rows
        out[:, g * 128:(g + 1) * 128] = word.astype(jnp.int16)


def encode(x):
    top = jnp.maximum(jnp.max(jnp.abs(x), axis=0, keepdims=True), 1e-30)
    level = jnp.ceil(jnp.log2(top) * 65536.0).astype(I32) + 4
    scale = TOP / jnp.exp2(level.astype(F32) * (1.0 / 65536.0))
    code = rounded(jnp.clip(x * scale, -TOP, TOP))
    mid = x.shape[0] // 2
    return pack(code[:mid], code[mid:]), level


def decode(w, rank):
    rows = rank // 2
    a, b = unpack(w[:rows, :])
    scale = jnp.exp2(w[rows:rows + 1, :].astype(F32) * (1.0 / 65536.0)) * (1.0 / TOP)
    return jnp.concatenate([a, b], axis=0) * scale


def errors_and_items(q, here, cols, left, left_t, values, t, err, right):
    q_hi, q_lo = split(q)
    right[0, :, here] = q_hi
    right[1, :, here] = q_lo
    guess = mm(left[0], q_hi) + mm(left[0], q_lo) + mm(left[1], q_hi)
    v = (lax.shift_right_logical(values[:, cols].astype(I32), 3 * t) & 7).astype(F32)
    e_hi, e_lo = split(jnp.where(v > 0, v - guess, 0.0))
    err[0, :, here] = e_hi
    err[1, :, here] = e_lo
    grad = mm(left_t[0], e_hi) + mm(left_t[0], e_lo) + mm(left_t[1], e_hi)
    return KEEP * q + learn_rate * grad


def first_items(dealt, meta, cols):
    w = dealt[cols, :].T
    a, b = unpack(w)
    return log_value(jnp.concatenate([a, b], axis=0), meta[0:1, 0:1])


CHUNK = 256


def my_turn(turn):
    return lax.rem(lax.axis_index("blk"), 2) == turn


def push_kernel(turn, t, half, left, left_t, values, *refs):
    source, (err, right, out) = refs[:-3], refs[-3:]
    wide = out.shape[1]

    @pl.when(my_turn(turn))
    def _():
        for at in range(0, wide, CHUNK):
            here = slice(at, at + CHUNK)
            cols = slice(half * wide + at, half * wide + at + CHUNK)
            if t == 0:
                q = first_items(*source, cols)
            else:
                q = decode(source[0][:, here], right.shape[1])
            new = errors_and_items(q, here, cols, left, left_t, values, t, err, right)
            words, level = encode(new)
            rows = words.shape[0]
            out[:rows, here] = words
            out[rows:, here] = jnp.broadcast_to(level, (out.shape[0] - rows, CHUNK))


def user_step(users, parts, rows=slice(None)):
    dims = ((1,), (1,))
    grad = None
    for err, right in parts:
        hi, lo = err[0, rows, :], err[1, rows, :]
        for a, b in ((hi, right[0]), (hi, right[1]), (lo, right[0])):
            term = mm(a, b, dims)
            grad = term if grad is None else grad + term
    return KEEP * users[rows, :] + learn_rate * grad


def pull_kernel(turn, users, err_a, right_a, err_b, right_b, new_users, left, left_t):
    @pl.when(my_turn(turn))
    def _():
        put_users(user_step(users, ((err_a, right_a), (err_b, right_b))), new_users, left, left_t)


def last_pull_kernel(*refs):
    outs = refs[10:]
    for turn, (users, *parts) in ((1, refs[:5]), (0, refs[5:10])):

        @pl.when(my_turn(turn))
        def _():
            put_users(user_step(users, (parts[:2], parts[2:])), *outs)


def last_items(half, left, left_t, values, got_o, got_e, items_out, err, right, held, sems):
    wide = right.shape[2]
    live = right.shape[1] // 2 + 8
    is_odd = my_turn(1)
    copies = []
    for at in range(0, wide, CHUNK):
        here = slice(at, at + CHUNK)
        cols = slice(half * wide + at, half * wide + at + CHUNK)
        q = decode(jnp.where(is_odd, got_o[:live, here], got_e[:live, here]), right.shape[1])
        held[here, :] = errors_and_items(q, here, cols, left, left_t, values, ROUNDS - 1, err, right).T
        copies.append(pltpu.make_async_copy(held.at[here, :], items_out.at[cols, :], sems.at[len(copies)]))
        copies[-1].start()
    return copies


def last_first_kernel(left, left_t, values, got_o, got_e, items_out, err, right, held, sems):
    for copy in last_items(0, left, left_t, values, got_o, got_e, items_out, err, right, held, sems):
        copy.wait()


def last_second_kernel(
    left, left_t, values, got_o, got_e, users, err_a, right_a, items_in,
    items_out, users_out, err, right, held, users_held, sems,
):
    copies = last_items(1, left, left_t, values, got_o, got_e, items_out, err, right, held, sems)
    tall = users_held.shape[0] // 2
    for at in (0, tall):
        rows = slice(at, at + tall)
        users_held[rows, :] = user_step(users, ((err_a, right_a), (err, right)), rows)
        copies.append(pltpu.make_async_copy(users_held.at[rows, :], users_out.at[rows, :], sems.at[len(copies)]))
        copies[-1].start()
    for copy in copies:
        copy.wait()


def struct(shape, dtype):
    return jax.ShapeDtypeStruct(shape, dtype)


def body(n_blk, item_content, projection, send_order, user_factors, ratings):
    n_users, rank = user_factors.shape
    n_items = send_order.shape[1]
    depth = item_content.shape[1]
    share = n_items // n_blk
    wide = n_items // 2
    part = lax.axis_index("cat")
    swap = [(0, 1), (1, 0)]
    away = lax.dynamic_slice_in_dim(item_content, (1 - part) * n_items, n_items, axis=0)
    came = [lax.ppermute(away[i * wide:(i + 1) * wide], "cat", swap) for i in range(2)]
    rows = 64
    groups = n_items // 128
    ratings = ratings.reshape(n_users, ROUNDS, groups, 128).transpose(0, 2, 1, 3)
    ratings = ratings.reshape(n_users * groups * ROUNDS, 128)
    values = pl.pallas_call(
        ratings_kernel,
        out_shape=struct((n_users, n_items), jnp.int16),
        grid=(n_users // rows,),
        in_specs=[pl.BlockSpec((rows * groups * ROUNDS, 128), lambda i: (i, 0))],
        out_specs=pl.BlockSpec((rows, n_items), lambda i: (i, 0)),
        compiler_params=params(52),
        cost_estimate=cost(1 << 20, 12 << 20),
        name="ratings",
    )(ratings)
    send_order, values = lax.optimization_barrier((send_order, values))
    split_shapes = [struct((2, n_users, rank), BF16), struct((2, rank, n_users), BF16)]
    deal, partial, meta, left, left_t = pl.pallas_call(
        before_kernel,
        out_shape=[
            struct((n_items, n_items), BF16),
            struct((n_items, rank), F32),
            struct((8, 128), F32),
        ] + split_shapes,
        in_specs=[VM, HBM, VM, HBM],
        out_specs=[VM] * 5,
        scratch_shapes=[
            pltpu.VMEM((n_items, depth), BF16),
            pltpu.VMEM((n_users, rank), F32),
            pltpu.SemaphoreType.DMA((2,)),
        ],
        compiler_params=params(),
        cost_estimate=cost(2 * n_items * n_items * depth, 6 << 20),
        name="before",
    )(send_order, item_content, projection, user_factors)
    coded = pl.pallas_call(
        project_kernel,
        out_shape=struct((n_items, rank // 2), I32),
        in_specs=[VM] * 6,
        out_specs=VM,
        compiler_params=params(),
        cost_estimate=cost(2 * n_items * n_items * depth, 4 << 20),
        name="project",
    )(deal, came[0], came[1], projection, partial, meta)
    dealt = lax.all_to_all(
        coded.reshape(n_blk, share, rank // 2), "blk", split_axis=0, concat_axis=0, tiled=True
    ).reshape(n_items, rank // 2)

    half_shapes = [struct((2, n_users, wide), BF16), struct((2, rank, wide), BF16)]
    to_even = [(i, (i + 1) % n_blk) for i in range(1, n_blk, 2)]
    to_odd = [(i, i ^ 1) for i in range(n_blk)]
    light = cost(1 << 10, 1 << 10)

    def push(turn, t, half, left, left_t, source, tail):
        *state, sent = pl.pallas_call(
            functools.partial(push_kernel, turn, t, half),
            out_shape=half_shapes + [struct((rank // 2 + tail, wide), I32)],
            in_specs=[VM] * (3 + len(source)),
            out_specs=[VM] * 3,
            compiler_params=params(),
            cost_estimate=light,
            name="push",
        )(left, left_t, values, *source)
        return state, sent

    def pull(turn, users, states):
        return pl.pallas_call(
            functools.partial(pull_kernel, turn),
            out_shape=[struct((n_users, rank), F32)] + split_shapes,
            in_specs=[VM] * 5,
            out_specs=[VM] * 3,
            compiler_params=params(),
            cost_estimate=light,
            name="pull",
        )(users, *states[0], *states[1])

    def after(x, done):
        return lax.optimization_barrier((x, done))[0]

    def both(turn, t, left, left_t, sources, tails, pairs):
        states, nexts = [], []
        for half in range(2):
            state, sent = push(turn, t, half, left, left_t, sources[half], tails[half])
            states.append(state)
            nexts.append([lax.ppermute(sent, "blk", pairs)])
            left = after(left, sent)
        return states, nexts, sent

    odd = even = (user_factors, left, left_t)
    for_odd = for_even = [[dealt, meta]] * 2
    even_states = None
    for t in range(ROUNDS - 1):
        odd_states, next_even, sent = both(1, t, *odd[1:], for_odd, EVEN_TAILS[t], to_even)
        if even_states is None:
            even = (even[0], after(even[1], sent), even[2])
        else:
            even = pull(0, after(even[0], sent), even_states)
        even_states, next_odd, _ = both(0, t, *even[1:], for_even, ODD_TAILS[t], to_odd)
        for_even, for_odd = next_even, next_odd
        if t < ROUNDS - 2:
            odd = pull(1, odd[0], odd_states)
    users, left, left_t = pl.pallas_call(
        last_pull_kernel,
        out_shape=[struct((n_users, rank), F32)] + split_shapes,
        in_specs=[VM] * 10,
        out_specs=[VM] * 3,
        compiler_params=params(),
        cost_estimate=light,
        name="last_pull",
    )(odd[0], *odd_states[0], *odd_states[1], even[0], *even_states[0], *even_states[1])

    anywhere = pl.BlockSpec(memory_space=pl.ANY)
    held_shapes = [pltpu.VMEM((wide, rank), F32)]
    items, err, right = pl.pallas_call(
        last_first_kernel,
        out_shape=[pltpu.HBM((n_items, rank), F32)] + half_shapes,
        in_specs=[VM] * 5,
        out_specs=[anywhere, VM, VM],
        scratch_shapes=held_shapes + [pltpu.SemaphoreType.DMA((wide // CHUNK,))],
        compiler_params=params(),
        cost_estimate=light,
        name="last_first",
    )(left, left_t, values, *for_odd[0], *for_even[0])
    items, users = pl.pallas_call(
        last_second_kernel,
        out_shape=[struct((n_items, rank), F32), struct((n_users, rank), F32)],
        in_specs=[VM] * 8 + [anywhere],
        out_specs=[anywhere] * 2,
        scratch_shapes=[
            pltpu.VMEM((2, n_users, wide), BF16),
            pltpu.VMEM((2, rank, wide), BF16),
        ] + held_shapes + [
            pltpu.VMEM((n_users, rank), F32),
            pltpu.SemaphoreType.DMA((wide // CHUNK + 2,)),
        ],
        input_output_aliases={8: 0},
        compiler_params=params(16),
        cost_estimate=light,
        name="last_second",
    )(left, left_t, values, *for_odd[1], *for_even[1], users, err, right, items)
    return users, items


def solution(mesh):
    placed = (
        P("blk", "cat"),
        P(),
        P(("blk", "cat"), None),
        P(("blk", "cat"), None),
        P(("blk", "cat"), None, None),
    )
    return jax.shard_map(
        functools.partial(body, mesh.shape["blk"]),
        mesh=mesh,
        in_specs=placed,
        out_specs=(P(("blk", "cat"), None), P(("blk", "cat"), None)),
        check_vma=False,
    )
```

```python
import functools

import jax
import jax.numpy as jnp
from jax import lax
from jax.experimental import pallas as pl
from jax.experimental.pallas import tpu as pltpu
from jax.sharding import PartitionSpec as P

ROUNDS = 4
learn_rate = 0.004
shrink = 0.05
KEEP = 1.0 - learn_rate * shrink
CONTENT_BOUND = 6.0
LOG_RANGE = 14.0
TOP = 32767.0
EVEN_TAIL = 16
ODD_TAIL = 8
F32 = jnp.float32
BF16 = jnp.bfloat16
I32 = jnp.int32

VM = pl.BlockSpec(memory_space=pltpu.VMEM)
HBM = pl.BlockSpec(memory_space=pltpu.HBM)


def params(limit=12):
    return pltpu.CompilerParams(vmem_limit_bytes=limit << 20)


def cost(flops, moved):
    return pl.CostEstimate(flops=flops, bytes_accessed=moved, transcendentals=0)


def split(x):
    hi = x.astype(BF16)
    return hi, (x - hi.astype(F32)).astype(BF16)


def mm(a, b, dims=((1,), (0,))):
    return lax.dot_general(a, b, (dims, ((), ())), preferred_element_type=F32)


def pack(a, b):
    return lax.shift_left(a, 16) | (b & 0xFFFF)


def unpack(w):
    return (
        lax.shift_right_arithmetic(w, 16).astype(F32),
        lax.shift_right_arithmetic(lax.shift_left(w, 16), 16).astype(F32),
    )


def rounded(x):
    return jnp.round(x).astype(I32)


def log_scale(bound):
    floor = bound * (2.0 ** -LOG_RANGE)
    return floor, TOP / (jnp.log2(1.0 + 2.0 ** LOG_RANGE) * 1.0001)


def log_code(x, bound):
    floor, scale = log_scale(bound)
    size = jnp.minimum(jnp.log2(1.0 + jnp.abs(x) / floor) * scale, TOP)
    return rounded(jnp.where(x < 0, -size, size))


def log_value(code, bound):
    floor, scale = log_scale(bound)
    size = (jnp.exp2(jnp.abs(code) * (1.0 / scale)) - 1.0) * floor
    return jnp.where(code < 0, -size, size)


def put_users(p, users, left, left_t):
    hi, lo = split(p)
    if users is not None:
        users[...] = p
    left[0] = hi
    left[1] = lo
    hi_t, lo_t = split(p.T)
    left_t[0] = hi_t
    left_t[1] = lo_t


def before_kernel(order, content, weights, users, deal, partial, meta, left, left_t, rows, held, sems):
    n = order.shape[1]
    part = lax.axis_index("cat")
    copy = pltpu.make_async_copy(content.at[pl.ds(pl.multiple_of(part * n, n), n), :], rows, sems.at[0])
    copy.start()
    users_copy = pltpu.make_async_copy(users, held, sems.at[1])
    users_copy.start()
    column_sums = jnp.sum(jnp.abs(weights[...].astype(F32)), axis=0, keepdims=True)
    bound = jnp.maximum(jnp.max(column_sums, axis=1, keepdims=True) * (CONTENT_BOUND * 1.001), 1e-30)
    meta[...] = jnp.broadcast_to(bound, meta.shape)
    lanes = lax.broadcasted_iota(I32, (128, n), 1)
    for at in range(0, n, 128):
        wide = jnp.broadcast_to(order[:, at:at + 128], (128, 128)).T
        picked = jnp.concatenate([wide] * (n // 128), axis=1) == lanes
        deal[at:at + 128, :] = jnp.where(picked, 1.0, 0.0).astype(BF16)
    users_copy.wait()
    put_users(held[...], None, left, left_t)
    copy.wait()
    depth = content.shape[1]
    mine = weights[pl.ds(pl.multiple_of(part * depth, depth), depth), :]
    partial[...] = mm(mm(deal[...], rows[...]).astype(BF16), mine)


def project_kernel(deal, first, second, weights, partial, meta, out):
    other = 1 - lax.axis_index("cat")
    depth = first.shape[1]
    half = first.shape[0]
    theirs = weights[pl.ds(pl.multiple_of(other * depth, depth), depth), :]
    rows = mm(deal[:, :half], first[...]) + mm(deal[:, half:], second[...])
    x = partial[...] + mm(rows.astype(BF16), theirs)
    code = log_code(x, meta[0:1, 0:1])
    mid = x.shape[1] // 2
    out[...] = pack(code[:, :mid], code[:, mid:])


def ratings_kernel(ratings, out):
    n, wide = out.shape
    groups = wide // 128
    for g in range(groups):
        word = None
        for t in reversed(range(ROUNDS)):
            rows = ratings[pl.ds(g * ROUNDS + t, n, stride=groups * ROUNDS), :]
            word = rows if word is None else lax.shift_left(word, 3) | rows
        out[:, g * 128:(g + 1) * 128] = word.astype(jnp.int16)


def encode(x):
    top = jnp.maximum(jnp.max(jnp.abs(x), axis=0, keepdims=True), 1e-30)
    level = jnp.ceil(jnp.log2(top) * 65536.0).astype(I32) + 4
    scale = TOP / jnp.exp2(level.astype(F32) * (1.0 / 65536.0))
    code = rounded(jnp.clip(x * scale, -TOP, TOP))
    mid = x.shape[0] // 2
    return pack(code[:mid], code[mid:]), level


def decode(w, rank):
    rows = rank // 2
    a, b = unpack(w[:rows, :])
    scale = jnp.exp2(w[rows:rows + 1, :].astype(F32) * (1.0 / 65536.0)) * (1.0 / TOP)
    return jnp.concatenate([a, b], axis=0) * scale


def errors_and_items(q, here, left, left_t, values, t, err, right):
    q_hi, q_lo = split(q)
    right[0, :, here] = q_hi
    right[1, :, here] = q_lo
    guess = mm(left[0], q_hi) + mm(left[0], q_lo) + mm(left[1], q_hi)
    v = (lax.shift_right_logical(values[:, here].astype(I32), 3 * t) & 7).astype(F32)
    e_hi, e_lo = split(jnp.where(v > 0, v - guess, 0.0))
    err[0, :, here] = e_hi
    err[1, :, here] = e_lo
    grad = mm(left_t[0], e_hi) + mm(left_t[0], e_lo) + mm(left_t[1], e_hi)
    return KEEP * q + learn_rate * grad


def first_items(dealt, meta, cols):
    w = dealt[cols, :].T
    a, b = unpack(w)
    return log_value(jnp.concatenate([a, b], axis=0), meta[0:1, 0:1])


CHUNK = 256


def my_turn(turn):
    return lax.rem(lax.axis_index("blk"), 2) == turn


def push_kernel(turn, t, left, left_t, values, *refs):
    source, (err, right, out) = refs[:-3], refs[-3:]
    wide = out.shape[1]

    @pl.when(my_turn(turn))
    def _():
        for at in range(0, wide, CHUNK):
            here = slice(at, at + CHUNK)
            if t == 0:
                q = first_items(*source, here)
            else:
                q = decode(source[0][:, here], right.shape[1])
            new = errors_and_items(q, here, left, left_t, values, t, err, right)
            words, level = encode(new)
            rows = words.shape[0]
            out[:rows, here] = words
            out[rows:, here] = jnp.broadcast_to(level, (out.shape[0] - rows, CHUNK))


def user_step(users, err, right, rows=slice(None)):
    dims = ((1,), (1,))
    hi, lo = err[0, rows, :], err[1, rows, :]
    grad = mm(hi, right[0], dims) + mm(hi, right[1], dims) + mm(lo, right[0], dims)
    return KEEP * users[rows, :] + learn_rate * grad


def pull_kernel(users, err_o, right_o, err_e, right_e, *outs):
    for turn, err, right in ((1, err_o, right_o), (0, err_e, right_e)):

        @pl.when(my_turn(turn))
        def _():
            put_users(user_step(users, err, right), *outs)


def last_kernel(left, left_t, values, users, got_o, got_e, items_out, users_out, err, right, held, users_held, sems):
    live = right.shape[1] // 2 + 8
    tall = users_held.shape[0] // 2
    is_odd = my_turn(1)
    copies = []

    def put(source, target, rows):
        copies.append(pltpu.make_async_copy(source.at[rows, :], target.at[rows, :], sems.at[len(copies)]))
        copies[-1].start()

    for at in range(0, right.shape[2], CHUNK):
        here = slice(at, at + CHUNK)
        q = decode(jnp.where(is_odd, got_o[:live, here], got_e[:live, here]), right.shape[1])
        held[here, :] = errors_and_items(q, here, left, left_t, values, ROUNDS - 1, err, right).T
        put(held, items_out, here)
    for at in (0, tall):
        rows = slice(at, at + tall)
        users_held[rows, :] = user_step(users, err, right, rows)
        put(users_held, users_out, rows)
    for copy in copies:
        copy.wait()


def struct(shape, dtype):
    return jax.ShapeDtypeStruct(shape, dtype)


def body(n_blk, item_content, projection, send_order, user_factors, ratings):
    n_users, rank = user_factors.shape
    n_items = send_order.shape[1]
    depth = item_content.shape[1]
    share = n_items // n_blk
    wide = n_items // 2
    part = lax.axis_index("cat")
    swap = [(0, 1), (1, 0)]
    away = lax.dynamic_slice_in_dim(item_content, (1 - part) * n_items, n_items, axis=0)
    came = [lax.ppermute(away[i * wide:(i + 1) * wide], "cat", swap) for i in range(2)]
    rows = 64
    groups = n_items // 128
    ratings = ratings.reshape(n_users, ROUNDS, groups, 128).transpose(0, 2, 1, 3)
    ratings = ratings.reshape(n_users * groups * ROUNDS, 128)
    values = pl.pallas_call(
        ratings_kernel,
        out_shape=struct((n_users, n_items), jnp.int16),
        grid=(n_users // rows,),
        in_specs=[pl.BlockSpec((rows * groups * ROUNDS, 128), lambda i: (i, 0))],
        out_specs=pl.BlockSpec((rows, n_items), lambda i: (i, 0)),
        compiler_params=params(52),
        cost_estimate=cost(1 << 20, 12 << 20),
        name="ratings",
    )(ratings)
    send_order, values = lax.optimization_barrier((send_order, values))
    split_shapes = [struct((2, n_users, rank), BF16), struct((2, rank, n_users), BF16)]
    deal, partial, meta, left, left_t = pl.pallas_call(
        before_kernel,
        out_shape=[
            struct((n_items, n_items), BF16),
            struct((n_items, rank), F32),
            struct((8, 128), F32),
        ] + split_shapes,
        in_specs=[VM, HBM, VM, HBM],
        out_specs=[VM] * 5,
        scratch_shapes=[
            pltpu.VMEM((n_items, depth), BF16),
            pltpu.VMEM((n_users, rank), F32),
            pltpu.SemaphoreType.DMA((2,)),
        ],
        compiler_params=params(),
        cost_estimate=cost(2 * n_items * n_items * depth, 6 << 20),
        name="before",
    )(send_order, item_content, projection, user_factors)
    coded = pl.pallas_call(
        project_kernel,
        out_shape=struct((n_items, rank // 2), I32),
        in_specs=[VM] * 6,
        out_specs=VM,
        compiler_params=params(),
        cost_estimate=cost(2 * n_items * n_items * depth, 4 << 20),
        name="project",
    )(deal, came[0], came[1], projection, partial, meta)
    dealt = lax.all_to_all(
        coded.reshape(n_blk, share, rank // 2), "blk", split_axis=0, concat_axis=0, tiled=True
    ).reshape(n_items, rank // 2)

    state_shapes = [struct((2, n_users, n_items), BF16), struct((2, rank, n_items), BF16)]
    ring = [(i, (i + 1) % n_blk) for i in range(n_blk)]
    pair = [(i, i ^ 1) for i in range(n_blk)]
    light = cost(1 << 10, 1 << 10)

    def push(turn, t, left, source, tail):
        *state, sent = pl.pallas_call(
            functools.partial(push_kernel, turn, t),
            out_shape=state_shapes + [struct((rank // 2 + tail, n_items), I32)],
            in_specs=[VM] * (3 + len(source)),
            out_specs=[VM] * 3,
            compiler_params=params(),
            cost_estimate=light,
            name="push",
        )(left, left_t, values, *source)
        return state, sent

    users = user_factors
    for_odd = for_even = [dealt, meta]
    for t in range(ROUNDS - 1):
        odd_state, sent = push(1, t, left, for_odd, EVEN_TAIL)
        next_even = [lax.ppermute(sent, "blk", ring)]
        later, _ = lax.optimization_barrier((left, sent))
        even_state, sent = push(0, t, later, for_even, ODD_TAIL)
        next_odd = [lax.ppermute(sent, "blk", pair)]
        users, left, left_t = pl.pallas_call(
            pull_kernel,
            out_shape=[struct((n_users, rank), F32)] + split_shapes,
            in_specs=[VM] * 5,
            out_specs=[VM] * 3,
            compiler_params=params(),
            cost_estimate=light,
            name="pull",
        )(users, *odd_state, *even_state)
        for_even, for_odd = next_even, next_odd

    anywhere = pl.BlockSpec(memory_space=pl.ANY)
    items, users = pl.pallas_call(
        last_kernel,
        out_shape=[struct((n_items, rank), F32), struct((n_users, rank), F32)],
        in_specs=[VM] * 6,
        out_specs=[anywhere] * 2,
        scratch_shapes=[
            pltpu.VMEM((2, n_users, n_items), BF16),
            pltpu.VMEM((2, rank, n_items), BF16),
            pltpu.VMEM((n_items, rank), F32),
            pltpu.VMEM((n_users, rank), F32),
            pltpu.SemaphoreType.DMA((n_items // CHUNK + 2,)),
        ],
        compiler_params=params(16),
        cost_estimate=light,
        name="last",
    )(left, left_t, values, users, *for_odd, *for_even)
    return users, items


def solution(mesh):
    placed = (
        P("blk", "cat"),
        P(),
        P(("blk", "cat"), None),
        P(("blk", "cat"), None),
        P(("blk", "cat"), None, None),
    )
    return jax.shard_map(
        functools.partial(body, mesh.shape["blk"]),
        mesh=mesh,
        in_specs=placed,
        out_specs=(P(("blk", "cat"), None), P(("blk", "cat"), None)),
        check_vma=False,
    )
```

```python
import functools

import jax
import jax.numpy as jnp
from jax import lax
from jax.experimental import pallas as pl
from jax.experimental.pallas import tpu as pltpu
from jax.sharding import PartitionSpec as P

ROUNDS = 4
learn_rate = 0.004
shrink = 0.05
KEEP = 1.0 - learn_rate * shrink
CONTENT_BOUND = 6.0
LOG_RANGE = 14.0
TOP = 32767.0
EVEN_TAIL = 16
ODD_TAIL = 8
F32 = jnp.float32
BF16 = jnp.bfloat16
I32 = jnp.int32

VM = pl.BlockSpec(memory_space=pltpu.VMEM)
HBM = pl.BlockSpec(memory_space=pltpu.HBM)


def params(limit=12):
    return pltpu.CompilerParams(vmem_limit_bytes=limit << 20)


def cost(flops, moved):
    return pl.CostEstimate(flops=flops, bytes_accessed=moved, transcendentals=0)


def split(x):
    hi = x.astype(BF16)
    return hi, (x - hi.astype(F32)).astype(BF16)


def mm(a, b, dims=((1,), (0,))):
    return lax.dot_general(a, b, (dims, ((), ())), preferred_element_type=F32)


def pack(a, b):
    return lax.shift_left(a, 16) | (b & 0xFFFF)


def unpack(w):
    return (
        lax.shift_right_arithmetic(w, 16).astype(F32),
        lax.shift_right_arithmetic(lax.shift_left(w, 16), 16).astype(F32),
    )


def rounded(x):
    return jnp.round(x).astype(I32)


def log_scale(bound):
    floor = bound * (2.0 ** -LOG_RANGE)
    return floor, TOP / (jnp.log2(1.0 + 2.0 ** LOG_RANGE) * 1.0001)


def log_code(x, bound):
    floor, scale = log_scale(bound)
    size = jnp.minimum(jnp.log2(1.0 + jnp.abs(x) / floor) * scale, TOP)
    return rounded(jnp.where(x < 0, -size, size))


def log_value(code, bound):
    floor, scale = log_scale(bound)
    size = (jnp.exp2(jnp.abs(code) * (1.0 / scale)) - 1.0) * floor
    return jnp.where(code < 0, -size, size)


def put_users(p, users, left, left_t):
    hi, lo = split(p)
    if users is not None:
        users[...] = p
    left[0] = hi
    left[1] = lo
    hi_t, lo_t = split(p.T)
    left_t[0] = hi_t
    left_t[1] = lo_t


def before_kernel(order, content, weights, users, deal, partial, meta, left, left_t, rows, held, sems):
    n = order.shape[1]
    part = lax.axis_index("cat")
    copy = pltpu.make_async_copy(content.at[pl.ds(pl.multiple_of(part * n, n), n), :], rows, sems.at[0])
    copy.start()
    users_copy = pltpu.make_async_copy(users, held, sems.at[1])
    users_copy.start()
    column_sums = jnp.sum(jnp.abs(weights[...].astype(F32)), axis=0, keepdims=True)
    bound = jnp.maximum(jnp.max(column_sums, axis=1, keepdims=True) * (CONTENT_BOUND * 1.001), 1e-30)
    meta[...] = jnp.broadcast_to(bound, meta.shape)
    lanes = lax.broadcasted_iota(I32, (128, n), 1)
    for at in range(0, n, 128):
        wide = jnp.broadcast_to(order[:, at:at + 128], (128, 128)).T
        picked = jnp.concatenate([wide] * (n // 128), axis=1) == lanes
        deal[at:at + 128, :] = jnp.where(picked, 1.0, 0.0).astype(BF16)
    users_copy.wait()
    put_users(held[...], None, left, left_t)
    copy.wait()
    depth = content.shape[1]
    mine = weights[pl.ds(pl.multiple_of(part * depth, depth), depth), :]
    partial[...] = mm(mm(deal[...], rows[...]).astype(BF16), mine)


def project_kernel(deal, first, second, weights, partial, meta, out):
    other = 1 - lax.axis_index("cat")
    depth = first.shape[1]
    half = first.shape[0]
    theirs = weights[pl.ds(pl.multiple_of(other * depth, depth), depth), :]
    rows = mm(deal[:, :half], first[...]) + mm(deal[:, half:], second[...])
    x = partial[...] + mm(rows.astype(BF16), theirs)
    code = log_code(x, meta[0:1, 0:1])
    mid = x.shape[1] // 2
    out[...] = pack(code[:, :mid], code[:, mid:])


def ratings_kernel(ratings, out):
    n, wide = out.shape
    groups = wide // 128
    for g in range(groups):
        word = None
        for t in reversed(range(ROUNDS)):
            rows = ratings[pl.ds(g * ROUNDS + t, n, stride=groups * ROUNDS), :]
            word = rows if word is None else lax.shift_left(word, 3) | rows
        out[:, g * 128:(g + 1) * 128] = word.astype(jnp.int16)


def encode(x):
    top = jnp.maximum(jnp.max(jnp.abs(x), axis=0, keepdims=True), 1e-30)
    level = jnp.ceil(jnp.log2(top) * 65536.0).astype(I32) + 4
    scale = TOP / jnp.exp2(level.astype(F32) * (1.0 / 65536.0))
    code = rounded(jnp.clip(x * scale, -TOP, TOP))
    mid = x.shape[0] // 2
    return pack(code[:mid], code[mid:]), level


def decode(w, rank):
    rows = rank // 2
    a, b = unpack(w[:rows, :])
    scale = jnp.exp2(w[rows:rows + 1, :].astype(F32) * (1.0 / 65536.0)) * (1.0 / TOP)
    return jnp.concatenate([a, b], axis=0) * scale


def errors_and_items(q, here, left, left_t, values, t, err, right, cols=None):
    q_hi, q_lo = split(q)
    right[0, :, here] = q_hi
    right[1, :, here] = q_lo
    guess = mm(left[0], q_hi) + mm(left[0], q_lo) + mm(left[1], q_hi)
    v = (lax.shift_right_logical(values[:, here if cols is None else cols].astype(I32), 3 * t) & 7).astype(F32)
    e_hi, e_lo = split(jnp.where(v > 0, v - guess, 0.0))
    err[0, :, here] = e_hi
    err[1, :, here] = e_lo
    grad = mm(left_t[0], e_hi) + mm(left_t[0], e_lo) + mm(left_t[1], e_hi)
    return KEEP * q + learn_rate * grad


def first_items(dealt, meta, cols):
    w = dealt[cols, :].T
    a, b = unpack(w)
    return log_value(jnp.concatenate([a, b], axis=0), meta[0:1, 0:1])


CHUNK = 256


def my_turn(turn):
    return lax.rem(lax.axis_index("blk"), 2) == turn


def n_source(t):
    return 2 if t == 0 else 1


def push_kernel(turn, t, left, left_t, values, *refs):
    count = n_source(t)
    source, err, right, outs = refs[:count], refs[count], refs[count + 1], refs[count + 2:]
    wide = outs[0].shape[1]

    @pl.when(my_turn(turn))
    def _():
        for at in range(0, wide * len(outs), CHUNK):
            here = slice(at, at + CHUNK)
            if t == 0:
                q = first_items(*source, here)
            else:
                q = decode(source[0][:, here], right.shape[1])
            new = errors_and_items(q, here, left, left_t, values, t, err, right)
            words, level = encode(new)
            rows = words.shape[0]
            out, there = outs[at // wide], slice(at % wide, at % wide + CHUNK)
            out[:rows, there] = words
            out[rows:, there] = jnp.broadcast_to(level, (out.shape[0] - rows, CHUNK))


def user_grad(err, right, rows):
    dims = ((1,), (1,))
    hi, lo = err[0, rows, :], err[1, rows, :]
    return mm(hi, right[0], dims) + mm(hi, right[1], dims) + mm(lo, right[0], dims)


def pull_kernel(users, err_o, right_o, err_e, right_e, *outs):
    for turn, err, right in ((1, err_o, right_o), (0, err_e, right_e)):

        @pl.when(my_turn(turn))
        def _():
            grad = user_grad(err, right, slice(None))
            put_users(KEEP * users[...] + learn_rate * grad, *outs)


def last_items(half, left, left_t, values, got_o, got_e, items_out, err, right, held, sems):
    wide = right.shape[2]
    live = right.shape[1] // 2 + 8
    is_odd = my_turn(1)
    copies = []
    for at in range(0, wide, CHUNK):
        here = slice(at, at + CHUNK)
        cols = slice(half * wide + at, half * wide + at + CHUNK)
        q = decode(jnp.where(is_odd, got_o[:live, here], got_e[:live, here]), right.shape[1])
        held[here, :] = errors_and_items(q, here, left, left_t, values, ROUNDS - 1, err, right, cols).T
        copies.append(pltpu.make_async_copy(held.at[here, :], items_out.at[cols, :], sems.at[len(copies)]))
        copies[-1].start()
    return copies


def last_first_kernel(left, left_t, values, users, got_o, got_e, items_out, part, err, right, held, sems):
    copies = last_items(0, left, left_t, values, got_o, got_e, items_out, err, right, held, sems)
    part[...] = KEEP * users[...] + learn_rate * user_grad(err, right, slice(None))
    for copy in copies:
        copy.wait()


def last_second_kernel(
    left, left_t, values, part, got_o, got_e, items_in, items_out, users_out, err, right, held, users_held, sems,
):
    copies = last_items(1, left, left_t, values, got_o, got_e, items_out, err, right, held, sems)
    tall = users_held.shape[0] // 2
    for at in (0, tall):
        rows = slice(at, at + tall)
        users_held[rows, :] = part[rows, :] + learn_rate * user_grad(err, right, rows)
        copies.append(pltpu.make_async_copy(users_held.at[rows, :], users_out.at[rows, :], sems.at[len(copies)]))
        copies[-1].start()
    for copy in copies:
        copy.wait()


def struct(shape, dtype):
    return jax.ShapeDtypeStruct(shape, dtype)


def body(n_blk, item_content, projection, send_order, user_factors, ratings):
    n_users, rank = user_factors.shape
    n_items = send_order.shape[1]
    depth = item_content.shape[1]
    share = n_items // n_blk
    wide = n_items // 2
    part = lax.axis_index("cat")
    swap = [(0, 1), (1, 0)]
    away = lax.dynamic_slice_in_dim(item_content, (1 - part) * n_items, n_items, axis=0)
    came = [lax.ppermute(away[i * wide:(i + 1) * wide], "cat", swap) for i in range(2)]
    rows = 64
    groups = n_items // 128
    ratings = ratings.reshape(n_users, ROUNDS, groups, 128).transpose(0, 2, 1, 3)
    ratings = ratings.reshape(n_users * groups * ROUNDS, 128)
    values = pl.pallas_call(
        ratings_kernel,
        out_shape=struct((n_users, n_items), jnp.int16),
        grid=(n_users // rows,),
        in_specs=[pl.BlockSpec((rows * groups * ROUNDS, 128), lambda i: (i, 0))],
        out_specs=pl.BlockSpec((rows, n_items), lambda i: (i, 0)),
        compiler_params=params(52),
        cost_estimate=cost(1 << 20, 12 << 20),
        name="ratings",
    )(ratings)
    send_order, values = lax.optimization_barrier((send_order, values))
    split_shapes = [struct((2, n_users, rank), BF16), struct((2, rank, n_users), BF16)]
    deal, partial, meta, left, left_t = pl.pallas_call(
        before_kernel,
        out_shape=[
            struct((n_items, n_items), BF16),
            struct((n_items, rank), F32),
            struct((8, 128), F32),
        ] + split_shapes,
        in_specs=[VM, HBM, VM, HBM],
        out_specs=[VM] * 5,
        scratch_shapes=[
            pltpu.VMEM((n_items, depth), BF16),
            pltpu.VMEM((n_users, rank), F32),
            pltpu.SemaphoreType.DMA((2,)),
        ],
        compiler_params=params(),
        cost_estimate=cost(2 * n_items * n_items * depth, 6 << 20),
        name="before",
    )(send_order, item_content, projection, user_factors)
    coded = pl.pallas_call(
        project_kernel,
        out_shape=struct((n_items, rank // 2), I32),
        in_specs=[VM] * 6,
        out_specs=VM,
        compiler_params=params(),
        cost_estimate=cost(2 * n_items * n_items * depth, 4 << 20),
        name="project",
    )(deal, came[0], came[1], projection, partial, meta)
    dealt = lax.all_to_all(
        coded.reshape(n_blk, share, rank // 2), "blk", split_axis=0, concat_axis=0, tiled=True
    ).reshape(n_items, rank // 2)

    state_shapes = [struct((2, n_users, n_items), BF16), struct((2, rank, n_items), BF16)]
    ring = [(i, (i + 1) % n_blk) for i in range(n_blk)]
    pair = [(i, i ^ 1) for i in range(n_blk)]
    light = cost(1 << 10, 1 << 10)

    def push(turn, t, left, source, tail, pieces=1):
        err, right, *sent = pl.pallas_call(
            functools.partial(push_kernel, turn, t),
            out_shape=state_shapes + [struct((rank // 2 + tail, n_items // pieces), I32)] * pieces,
            in_specs=[VM] * (3 + len(source)),
            out_specs=[VM] * (2 + pieces),
            compiler_params=params(),
            cost_estimate=light,
            name="push",
        )(left, left_t, values, *source)
        return (err, right), sent

    users = user_factors
    for_odd = for_even = [dealt, meta]
    for t in range(ROUNDS - 1):
        pieces = 1 if t < ROUNDS - 2 else 2
        odd_state, sent = push(1, t, left, for_odd, EVEN_TAIL, pieces)
        next_even = [lax.ppermute(x, "blk", ring) for x in sent]
        later, _ = lax.optimization_barrier((left, sent[0]))
        even_state, sent = push(0, t, later, for_even, ODD_TAIL, pieces)
        next_odd = [lax.ppermute(x, "blk", pair) for x in sent]
        users, left, left_t = pl.pallas_call(
            pull_kernel,
            out_shape=[struct((n_users, rank), F32)] + split_shapes,
            in_specs=[VM] * 5,
            out_specs=[VM] * 3,
            compiler_params=params(),
            cost_estimate=light,
            name="pull",
        )(users, *odd_state, *even_state)
        for_even, for_odd = next_even, next_odd

    anywhere = pl.BlockSpec(memory_space=pl.ANY)
    scratch = [pltpu.VMEM((2, n_users, wide), BF16), pltpu.VMEM((2, rank, wide), BF16), pltpu.VMEM((wide, rank), F32)]
    items, part = pl.pallas_call(
        last_first_kernel,
        out_shape=[pltpu.HBM((n_items, rank), F32), struct((n_users, rank), F32)],
        in_specs=[VM] * 6,
        out_specs=[anywhere, VM],
        scratch_shapes=scratch + [pltpu.SemaphoreType.DMA((wide // CHUNK,))],
        compiler_params=params(),
        cost_estimate=light,
        name="last_first",
    )(left, left_t, values, users, for_odd[0], for_even[0])
    items, users = pl.pallas_call(
        last_second_kernel,
        out_shape=[struct((n_items, rank), F32), struct((n_users, rank), F32)],
        in_specs=[VM] * 6 + [anywhere],
        out_specs=[anywhere] * 2,
        scratch_shapes=scratch + [
            pltpu.VMEM((n_users, rank), F32),
            pltpu.SemaphoreType.DMA((wide // CHUNK + 2,)),
        ],
        input_output_aliases={6: 0},
        compiler_params=params(),
        cost_estimate=light,
        name="last_second",
    )(left, left_t, values, part, for_odd[1], for_even[1], items)
    return users, items


def solution(mesh):
    placed = (
        P("blk", "cat"),
        P(),
        P(("blk", "cat"), None),
        P(("blk", "cat"), None),
        P(("blk", "cat"), None, None),
    )
    return jax.shard_map(
        functools.partial(body, mesh.shape["blk"]),
        mesh=mesh,
        in_specs=placed,
        out_specs=(P(("blk", "cat"), None), P(("blk", "cat"), None)),
        check_vma=False,
    )
```

```python
import functools

import jax
import jax.numpy as jnp
from jax import lax
from jax.experimental import pallas as pl
from jax.experimental.pallas import tpu as pltpu
from jax.sharding import PartitionSpec as P

ROUNDS = 4
learn_rate = 0.004
shrink = 0.05
KEEP = 1.0 - learn_rate * shrink
CONTENT_BOUND = 6.0
LOG_RANGE = 14.0
TOP = 32767.0
EVEN_TAIL = 16
ODD_TAIL = 8
F32 = jnp.float32
BF16 = jnp.bfloat16
I32 = jnp.int32

VM = pl.BlockSpec(memory_space=pltpu.VMEM)
HBM = pl.BlockSpec(memory_space=pltpu.HBM)


def params(limit=12):
    return pltpu.CompilerParams(vmem_limit_bytes=limit << 20)


def cost(flops, moved):
    return pl.CostEstimate(flops=flops, bytes_accessed=moved, transcendentals=0)


def split(x):
    hi = x.astype(BF16)
    return hi, (x - hi.astype(F32)).astype(BF16)


def mm(a, b, dims=((1,), (0,))):
    return lax.dot_general(a, b, (dims, ((), ())), preferred_element_type=F32)


def pack(a, b):
    return lax.shift_left(a, 16) | (b & 0xFFFF)


def unpack(w):
    return (
        lax.shift_right_arithmetic(w, 16).astype(F32),
        lax.shift_right_arithmetic(lax.shift_left(w, 16), 16).astype(F32),
    )


def rounded(x):
    return jnp.round(x).astype(I32)


def log_scale(bound):
    floor = bound * (2.0 ** -LOG_RANGE)
    return floor, TOP / (jnp.log2(1.0 + 2.0 ** LOG_RANGE) * 1.0001)


def log_code(x, bound):
    floor, scale = log_scale(bound)
    size = jnp.minimum(jnp.log2(1.0 + jnp.abs(x) / floor) * scale, TOP)
    return rounded(jnp.where(x < 0, -size, size))


def log_value(code, bound):
    floor, scale = log_scale(bound)
    size = (jnp.exp2(jnp.abs(code) * (1.0 / scale)) - 1.0) * floor
    return jnp.where(code < 0, -size, size)


def put_users(p, users, left, left_t):
    if users is not None:
        users[...] = p
    for out, x in ((left, p), (left_t, p.T)):
        hi, lo = split(x)
        depth = x.shape[1]
        out[:, :depth] = hi
        out[:, depth:2 * depth] = hi
        out[:, 2 * depth:] = lo


def before_kernel(order, content, weights, users, deal, partial, meta, left, left_t, rows, held, sems):
    n = order.shape[1]
    part = lax.axis_index("cat")
    copy = pltpu.make_async_copy(content.at[pl.ds(pl.multiple_of(part * n, n), n), :], rows, sems.at[0])
    copy.start()
    users_copy = pltpu.make_async_copy(users, held, sems.at[1])
    users_copy.start()
    column_sums = jnp.sum(jnp.abs(weights[...].astype(F32)), axis=0, keepdims=True)
    bound = jnp.maximum(jnp.max(column_sums, axis=1, keepdims=True) * (CONTENT_BOUND * 1.001), 1e-30)
    meta[...] = jnp.broadcast_to(bound, meta.shape)
    lanes = lax.broadcasted_iota(I32, (128, n), 1)
    for at in range(0, n, 128):
        wide = jnp.broadcast_to(order[:, at:at + 128], (128, 128)).T
        picked = jnp.concatenate([wide] * (n // 128), axis=1) == lanes
        deal[at:at + 128, :] = jnp.where(picked, 1.0, 0.0).astype(BF16)
    users_copy.wait()
    put_users(held[...], None, left, left_t)
    copy.wait()
    depth = content.shape[1]
    mine = weights[pl.ds(pl.multiple_of(part * depth, depth), depth), :]
    partial[...] = mm(mm(deal[...], rows[...]).astype(BF16), mine)


def project_kernel(deal, first, second, weights, partial, meta, out):
    other = 1 - lax.axis_index("cat")
    depth = first.shape[1]
    half = first.shape[0]
    theirs = weights[pl.ds(pl.multiple_of(other * depth, depth), depth), :]
    rows = mm(deal[:, :half], first[...]) + mm(deal[:, half:], second[...])
    x = partial[...] + mm(rows.astype(BF16), theirs)
    code = log_code(x, meta[0:1, 0:1])
    mid = x.shape[1] // 2
    out[...] = pack(code[:, :mid], code[:, mid:])


def ratings_kernel(ratings, out):
    n, wide = out.shape
    groups = wide // 128
    for g in range(groups):
        word = None
        for t in reversed(range(ROUNDS)):
            rows = ratings[pl.ds(g * ROUNDS + t, n, stride=groups * ROUNDS), :]
            word = rows if word is None else lax.shift_left(word, 3) | rows
        out[:, g * 128:(g + 1) * 128] = word.astype(jnp.int16)


def encode(x):
    top = jnp.maximum(jnp.max(jnp.abs(x), axis=0, keepdims=True), 1e-30)
    level = jnp.ceil(jnp.log2(top) * 65536.0).astype(I32) + 4
    scale = TOP / jnp.exp2(level.astype(F32) * (1.0 / 65536.0))
    code = rounded(jnp.clip(x * scale, -TOP, TOP))
    mid = x.shape[0] // 2
    return pack(code[:mid], code[mid:]), level


def decode(w, rank):
    rows = rank // 2
    a, b = unpack(w[:rows, :])
    scale = jnp.exp2(w[rows:rows + 1, :].astype(F32) * (1.0 / 65536.0)) * (1.0 / TOP)
    return jnp.concatenate([a, b], axis=0) * scale


def errors_and_items(q, here, left, left_t, values, t, err, right, cols=None):
    q_hi, q_lo = split(q)
    right[0, :, here] = q_hi
    right[1, :, here] = q_lo
    guess = mm(left[...], jnp.concatenate([q_hi, q_lo, q_hi], axis=0))
    v = (lax.shift_right_logical(values[:, here if cols is None else cols].astype(I32), 3 * t) & 7).astype(F32)
    e_hi, e_lo = split(jnp.where(v > 0, v - guess, 0.0))
    err[0, :, here] = e_hi
    err[1, :, here] = e_lo
    grad = mm(left_t[...], jnp.concatenate([e_hi, e_lo, e_hi], axis=0))
    return KEEP * q + learn_rate * grad


def first_items(dealt, meta, cols):
    w = dealt[cols, :].T
    a, b = unpack(w)
    return log_value(jnp.concatenate([a, b], axis=0), meta[0:1, 0:1])


CHUNK = 256


def my_turn(turn):
    return lax.rem(lax.axis_index("blk"), 2) == turn


def n_source(t):
    return 2 if t == 0 else 1


def push_kernel(turn, t, left, left_t, values, *refs):
    count = n_source(t)
    source, err, right, outs = refs[:count], refs[count], refs[count + 1], refs[count + 2:]
    wide = outs[0].shape[1]

    @pl.when(my_turn(turn))
    def _():
        for at in range(0, wide * len(outs), CHUNK):
            here = slice(at, at + CHUNK)
            if t == 0:
                q = first_items(*source, here)
            else:
                q = decode(source[0][:, here], right.shape[1])
            new = errors_and_items(q, here, left, left_t, values, t, err, right)
            words, level = encode(new)
            rows = words.shape[0]
            out, there = outs[at // wide], slice(at % wide, at % wide + CHUNK)
            out[:rows, there] = words
            out[rows:, there] = jnp.broadcast_to(level, (out.shape[0] - rows, CHUNK))


def user_grad(err, right, rows):
    dims = ((1,), (1,))
    hi, lo = err[0, rows, :], err[1, rows, :]
    return mm(hi, right[0], dims) + mm(hi, right[1], dims) + mm(lo, right[0], dims)


def pull_kernel(users, err_o, right_o, err_e, right_e, *outs):
    for turn, err, right in ((1, err_o, right_o), (0, err_e, right_e)):

        @pl.when(my_turn(turn))
        def _():
            grad = user_grad(err, right, slice(None))
            put_users(KEEP * users[...] + learn_rate * grad, *outs)


def last_items(half, left, left_t, values, got_o, got_e, items_out, err, right, held, sems):
    wide = right.shape[2]
    live = right.shape[1] // 2 + 8
    is_odd = my_turn(1)
    copies = []
    for at in range(0, wide, CHUNK):
        here = slice(at, at + CHUNK)
        cols = slice(half * wide + at, half * wide + at + CHUNK)
        q = decode(jnp.where(is_odd, got_o[:live, here], got_e[:live, here]), right.shape[1])
        held[here, :] = errors_and_items(q, here, left, left_t, values, ROUNDS - 1, err, right, cols).T
        copies.append(pltpu.make_async_copy(held.at[here, :], items_out.at[cols, :], sems.at[len(copies)]))
        copies[-1].start()
    return copies


def last_first_kernel(left, left_t, values, users, got_o, got_e, items_out, part, err, right, held, sems):
    copies = last_items(0, left, left_t, values, got_o, got_e, items_out, err, right, held, sems)
    part[...] = KEEP * users[...] + learn_rate * user_grad(err, right, slice(None))
    for copy in copies:
        copy.wait()


def last_second_kernel(
    left, left_t, values, part, got_o, got_e, items_in, items_out, users_out, err, right, held, users_held, sems,
):
    copies = last_items(1, left, left_t, values, got_o, got_e, items_out, err, right, held, sems)
    tall = users_held.shape[0] // 2
    for at in (0, tall):
        rows = slice(at, at + tall)
        users_held[rows, :] = part[rows, :] + learn_rate * user_grad(err, right, rows)
        copies.append(pltpu.make_async_copy(users_held.at[rows, :], users_out.at[rows, :], sems.at[len(copies)]))
        copies[-1].start()
    for copy in copies:
        copy.wait()


def struct(shape, dtype):
    return jax.ShapeDtypeStruct(shape, dtype)


def body(n_blk, item_content, projection, send_order, user_factors, ratings):
    n_users, rank = user_factors.shape
    n_items = send_order.shape[1]
    depth = item_content.shape[1]
    share = n_items // n_blk
    wide = n_items // 2
    part = lax.axis_index("cat")
    swap = [(0, 1), (1, 0)]
    away = lax.dynamic_slice_in_dim(item_content, (1 - part) * n_items, n_items, axis=0)
    came = [lax.ppermute(away[i * wide:(i + 1) * wide], "cat", swap) for i in range(2)]
    rows = 64
    groups = n_items // 128
    ratings = ratings.reshape(n_users, ROUNDS, groups, 128).transpose(0, 2, 1, 3)
    ratings = ratings.reshape(n_users * groups * ROUNDS, 128)
    values = pl.pallas_call(
        ratings_kernel,
        out_shape=struct((n_users, n_items), jnp.int16),
        grid=(n_users // rows,),
        in_specs=[pl.BlockSpec((rows * groups * ROUNDS, 128), lambda i: (i, 0))],
        out_specs=pl.BlockSpec((rows, n_items), lambda i: (i, 0)),
        compiler_params=params(52),
        cost_estimate=cost(1 << 20, 12 << 20),
        name="ratings",
    )(ratings)
    send_order, values = lax.optimization_barrier((send_order, values))
    split_shapes = [struct((n_users, 3 * rank), BF16), struct((rank, 3 * n_users), BF16)]
    deal, partial, meta, left, left_t = pl.pallas_call(
        before_kernel,
        out_shape=[
            struct((n_items, n_items), BF16),
            struct((n_items, rank), F32),
            struct((8, 128), F32),
        ] + split_shapes,
        in_specs=[VM, HBM, VM, HBM],
        out_specs=[VM] * 5,
        scratch_shapes=[
            pltpu.VMEM((n_items, depth), BF16),
            pltpu.VMEM((n_users, rank), F32),
            pltpu.SemaphoreType.DMA((2,)),
        ],
        compiler_params=params(),
        cost_estimate=cost(2 * n_items * n_items * depth, 6 << 20),
        name="before",
    )(send_order, item_content, projection, user_factors)
    coded = pl.pallas_call(
        project_kernel,
        out_shape=struct((n_items, rank // 2), I32),
        in_specs=[VM] * 6,
        out_specs=VM,
        compiler_params=params(),
        cost_estimate=cost(2 * n_items * n_items * depth, 4 << 20),
        name="project",
    )(deal, came[0], came[1], projection, partial, meta)
    dealt = lax.all_to_all(
        coded.reshape(n_blk, share, rank // 2), "blk", split_axis=0, concat_axis=0, tiled=True
    ).reshape(n_items, rank // 2)

    state_shapes = [struct((2, n_users, n_items), BF16), struct((2, rank, n_items), BF16)]
    ring = [(i, (i + 1) % n_blk) for i in range(n_blk)]
    pair = [(i, i ^ 1) for i in range(n_blk)]
    light = cost(1 << 10, 1 << 10)

    def push(turn, t, left, source, tail, pieces=1):
        err, right, *sent = pl.pallas_call(
            functools.partial(push_kernel, turn, t),
            out_shape=state_shapes + [struct((rank // 2 + tail, n_items // pieces), I32)] * pieces,
            in_specs=[VM] * (3 + len(source)),
            out_specs=[VM] * (2 + pieces),
            compiler_params=params(),
            cost_estimate=light,
            name="push",
        )(left, left_t, values, *source)
        return (err, right), sent

    users = user_factors
    for_odd = for_even = [dealt, meta]
    for t in range(ROUNDS - 1):
        pieces = 1 if t < ROUNDS - 2 else 2
        odd_state, sent = push(1, t, left, for_odd, EVEN_TAIL, pieces)
        next_even = [lax.ppermute(x, "blk", ring) for x in sent]
        later, _ = lax.optimization_barrier((left, sent[0]))
        even_state, sent = push(0, t, later, for_even, ODD_TAIL, pieces)
        next_odd = [lax.ppermute(x, "blk", pair) for x in sent]
        users, left, left_t = pl.pallas_call(
            pull_kernel,
            out_shape=[struct((n_users, rank), F32)] + split_shapes,
            in_specs=[VM] * 5,
            out_specs=[VM] * 3,
            compiler_params=params(),
            cost_estimate=light,
            name="pull",
        )(users, *odd_state, *even_state)
        for_even, for_odd = next_even, next_odd

    anywhere = pl.BlockSpec(memory_space=pl.ANY)
    scratch = [pltpu.VMEM((2, n_users, wide), BF16), pltpu.VMEM((2, rank, wide), BF16), pltpu.VMEM((wide, rank), F32)]
    items, part = pl.pallas_call(
        last_first_kernel,
        out_shape=[pltpu.HBM((n_items, rank), F32), struct((n_users, rank), F32)],
        in_specs=[VM] * 6,
        out_specs=[anywhere, VM],
        scratch_shapes=scratch + [pltpu.SemaphoreType.DMA((wide // CHUNK,))],
        compiler_params=params(),
        cost_estimate=light,
        name="last_first",
    )(left, left_t, values, users, for_odd[0], for_even[0])
    items, users = pl.pallas_call(
        last_second_kernel,
        out_shape=[struct((n_items, rank), F32), struct((n_users, rank), F32)],
        in_specs=[VM] * 6 + [anywhere],
        out_specs=[anywhere] * 2,
        scratch_shapes=scratch + [
            pltpu.VMEM((n_users, rank), F32),
            pltpu.SemaphoreType.DMA((wide // CHUNK + 2,)),
        ],
        input_output_aliases={6: 0},
        compiler_params=params(),
        cost_estimate=light,
        name="last_second",
    )(left, left_t, values, part, for_odd[1], for_even[1], items)
    return users, items


def solution(mesh):
    placed = (
        P("blk", "cat"),
        P(),
        P(("blk", "cat"), None),
        P(("blk", "cat"), None),
        P(("blk", "cat"), None, None),
    )
    return jax.shard_map(
        functools.partial(body, mesh.shape["blk"]),
        mesh=mesh,
        in_specs=placed,
        out_specs=(P(("blk", "cat"), None), P(("blk", "cat"), None)),
        check_vma=False,
    )
```

```python
import functools

import jax
import jax.numpy as jnp
from jax import lax
from jax.experimental import pallas as pl
from jax.experimental.pallas import tpu as pltpu
from jax.sharding import PartitionSpec as P

ROUNDS = 4
learn_rate = 0.004
shrink = 0.05
KEEP = 1.0 - learn_rate * shrink
CONTENT_BOUND = 6.0
LOG_RANGE = 14.0
TOP = 32767.0
EVEN_TAIL = 16
ODD_TAIL = 8
F32 = jnp.float32
BF16 = jnp.bfloat16
I32 = jnp.int32

VM = pl.BlockSpec(memory_space=pltpu.VMEM)
HBM = pl.BlockSpec(memory_space=pltpu.HBM)


def params(limit=12):
    return pltpu.CompilerParams(vmem_limit_bytes=limit << 20)


def cost(flops, moved):
    return pl.CostEstimate(flops=flops, bytes_accessed=moved, transcendentals=0)


def split(x):
    hi = x.astype(BF16)
    return hi, (x - hi.astype(F32)).astype(BF16)


def mm(a, b, dims=((1,), (0,))):
    return lax.dot_general(a, b, (dims, ((), ())), preferred_element_type=F32)


def pack(a, b):
    return lax.shift_left(a, 16) | (b & 0xFFFF)


def unpack(w):
    return (
        lax.shift_right_arithmetic(w, 16).astype(F32),
        lax.shift_right_arithmetic(lax.shift_left(w, 16), 16).astype(F32),
    )


def rounded(x):
    return jnp.round(x).astype(I32)


def log_scale(bound):
    floor = bound * (2.0 ** -LOG_RANGE)
    return floor, TOP / (jnp.log2(1.0 + 2.0 ** LOG_RANGE) * 1.0001)


def log_code(x, bound):
    floor, scale = log_scale(bound)
    size = jnp.minimum(jnp.log2(1.0 + jnp.abs(x) / floor) * scale, TOP)
    return rounded(jnp.where(x < 0, -size, size))


def log_value(code, bound):
    floor, scale = log_scale(bound)
    size = (jnp.exp2(jnp.abs(code) * (1.0 / scale)) - 1.0) * floor
    return jnp.where(code < 0, -size, size)


def put_users(p, users, left, left_t):
    hi, lo = split(p)
    if users is not None:
        users[...] = p
    left[0] = hi
    left[1] = lo
    hi_t, lo_t = split(p.T)
    left_t[0] = hi_t
    left_t[1] = lo_t


def before_kernel(order, content, weights, users, deal, partial, meta, left, left_t, rows, held, sems):
    n = order.shape[1]
    part = lax.axis_index("cat")
    copy = pltpu.make_async_copy(content.at[pl.ds(pl.multiple_of(part * n, n), n), :], rows, sems.at[0])
    copy.start()
    users_copy = pltpu.make_async_copy(users, held, sems.at[1])
    users_copy.start()
    column_sums = jnp.sum(jnp.abs(weights[...].astype(F32)), axis=0, keepdims=True)
    bound = jnp.maximum(jnp.max(column_sums, axis=1, keepdims=True) * (CONTENT_BOUND * 1.001), 1e-30)
    meta[...] = jnp.broadcast_to(bound, meta.shape)
    lanes = lax.broadcasted_iota(I32, (128, n), 1)
    for at in range(0, n, 128):
        wide = jnp.broadcast_to(order[:, at:at + 128], (128, 128)).T
        picked = jnp.concatenate([wide] * (n // 128), axis=1) == lanes
        deal[at:at + 128, :] = jnp.where(picked, 1.0, 0.0).astype(BF16)
    users_copy.wait()
    put_users(held[...], None, left, left_t)
    copy.wait()
    depth = content.shape[1]
    mine = weights[pl.ds(pl.multiple_of(part * depth, depth), depth), :]
    partial[...] = mm(mm(deal[...], rows[...]).astype(BF16), mine)


def project_kernel(deal, first, second, weights, partial, meta, out):
    other = 1 - lax.axis_index("cat")
    depth = first.shape[1]
    half = first.shape[0]
    theirs = weights[pl.ds(pl.multiple_of(other * depth, depth), depth), :]
    rows = mm(deal[:, :half], first[...]) + mm(deal[:, half:], second[...])
    x = partial[...] + mm(rows.astype(BF16), theirs)
    code = log_code(x, meta[0:1, 0:1])
    mid = x.shape[1] // 2
    out[...] = pack(code[:, :mid], code[:, mid:])


def ratings_kernel(ratings, out):
    n, wide = out.shape
    groups = wide // 128
    for g in range(groups):
        word = None
        for t in reversed(range(ROUNDS)):
            rows = ratings[pl.ds(g * ROUNDS + t, n, stride=groups * ROUNDS), :]
            word = rows if word is None else lax.shift_left(word, 3) | rows
        out[:, g * 128:(g + 1) * 128] = word.astype(jnp.int16)


def encode(x):
    top = jnp.maximum(jnp.max(jnp.abs(x), axis=0, keepdims=True), 1e-30)
    level = jnp.ceil(jnp.log2(top) * 65536.0).astype(I32) + 4
    scale = TOP / jnp.exp2(level.astype(F32) * (1.0 / 65536.0))
    code = rounded(jnp.clip(x * scale, -TOP, TOP))
    mid = x.shape[0] // 2
    return pack(code[:mid], code[mid:]), level


def decode(w, rank):
    rows = rank // 2
    a, b = unpack(w[:rows, :])
    scale = jnp.exp2(w[rows:rows + 1, :].astype(F32) * (1.0 / 65536.0)) * (1.0 / TOP)
    return jnp.concatenate([a, b], axis=0) * scale


def errors_and_items(q, here, left, left_t, values, t, err, right, cols=None):
    q_hi, q_lo = split(q)
    right[0, :, here] = q_hi
    right[1, :, here] = q_lo
    guess = mm(left[0], q_hi) + mm(left[0], q_lo) + mm(left[1], q_hi)
    v = (lax.shift_right_logical(values[:, here if cols is None else cols].astype(I32), 3 * t) & 7).astype(F32)
    e_hi, e_lo = split(jnp.where(v > 0, v - guess, 0.0))
    err[0, :, here] = e_hi
    err[1, :, here] = e_lo
    grad = mm(left_t[0], e_hi) + mm(left_t[0], e_lo) + mm(left_t[1], e_hi)
    return KEEP * q + learn_rate * grad


def first_items(dealt, meta, cols):
    w = dealt[cols, :].T
    a, b = unpack(w)
    return log_value(jnp.concatenate([a, b], axis=0), meta[0:1, 0:1])


CHUNK = 512


def my_turn(turn):
    return lax.rem(lax.axis_index("blk"), 2) == turn


def n_source(t):
    return 2 if t == 0 else 1


def push_kernel(turn, t, left, left_t, values, *refs):
    count = n_source(t)
    source, err, right, outs = refs[:count], refs[count], refs[count + 1], refs[count + 2:]
    wide = outs[0].shape[1]

    @pl.when(my_turn(turn))
    def _():
        for at in range(0, wide * len(outs), CHUNK):
            here = slice(at, at + CHUNK)
            if t == 0:
                q = first_items(*source, here)
            else:
                q = decode(source[0][:, here], right.shape[1])
            new = errors_and_items(q, here, left, left_t, values, t, err, right)
            words, level = encode(new)
            rows = words.shape[0]
            out, there = outs[at // wide], slice(at % wide, at % wide + CHUNK)
            out[:rows, there] = words
            out[rows:, there] = jnp.broadcast_to(level, (out.shape[0] - rows, CHUNK))


def user_grad(err, right, rows):
    dims = ((1,), (1,))
    hi, lo = err[0, rows, :], err[1, rows, :]
    return mm(hi, right[0], dims) + mm(hi, right[1], dims) + mm(lo, right[0], dims)


def pull_kernel(users, err_o, right_o, err_e, right_e, *outs):
    for turn, err, right in ((1, err_o, right_o), (0, err_e, right_e)):

        @pl.when(my_turn(turn))
        def _():
            grad = user_grad(err, right, slice(None))
            put_users(KEEP * users[...] + learn_rate * grad, *outs)


def last_items(half, left, left_t, values, got_o, got_e, items_out, err, right, held, sems):
    wide = right.shape[2]
    live = right.shape[1] // 2 + 8
    is_odd = my_turn(1)
    copies = []
    for at in range(0, wide, CHUNK):
        here = slice(at, at + CHUNK)
        cols = slice(half * wide + at, half * wide + at + CHUNK)
        q = decode(jnp.where(is_odd, got_o[:live, here], got_e[:live, here]), right.shape[1])
        held[here, :] = errors_and_items(q, here, left, left_t, values, ROUNDS - 1, err, right, cols).T
        copies.append(pltpu.make_async_copy(held.at[here, :], items_out.at[cols, :], sems.at[len(copies)]))
        copies[-1].start()
    return copies


def last_first_kernel(left, left_t, values, users, got_o, got_e, items_out, part, err, right, held, sems):
    copies = last_items(0, left, left_t, values, got_o, got_e, items_out, err, right, held, sems)
    part[...] = KEEP * users[...] + learn_rate * user_grad(err, right, slice(None))
    for copy in copies:
        copy.wait()


def last_second_kernel(
    left, left_t, values, part, got_o, got_e, items_in, items_out, users_out, err, right, held, users_held, sems,
):
    copies = last_items(1, left, left_t, values, got_o, got_e, items_out, err, right, held, sems)
    tall = users_held.shape[0] // 2
    for at in (0, tall):
        rows = slice(at, at + tall)
        users_held[rows, :] = part[rows, :] + learn_rate * user_grad(err, right, rows)
        copies.append(pltpu.make_async_copy(users_held.at[rows, :], users_out.at[rows, :], sems.at[len(copies)]))
        copies[-1].start()
    for copy in copies:
        copy.wait()


def struct(shape, dtype):
    return jax.ShapeDtypeStruct(shape, dtype)


def body(n_blk, item_content, projection, send_order, user_factors, ratings):
    n_users, rank = user_factors.shape
    n_items = send_order.shape[1]
    depth = item_content.shape[1]
    share = n_items // n_blk
    wide = n_items // 2
    part = lax.axis_index("cat")
    swap = [(0, 1), (1, 0)]
    away = lax.dynamic_slice_in_dim(item_content, (1 - part) * n_items, n_items, axis=0)
    came = [lax.ppermute(away[i * wide:(i + 1) * wide], "cat", swap) for i in range(2)]
    rows = 64
    groups = n_items // 128
    ratings = ratings.reshape(n_users, ROUNDS, groups, 128).transpose(0, 2, 1, 3)
    ratings = ratings.reshape(n_users * groups * ROUNDS, 128)
    values = pl.pallas_call(
        ratings_kernel,
        out_shape=struct((n_users, n_items), jnp.int16),
        grid=(n_users // rows,),
        in_specs=[pl.BlockSpec((rows * groups * ROUNDS, 128), lambda i: (i, 0))],
        out_specs=pl.BlockSpec((rows, n_items), lambda i: (i, 0)),
        compiler_params=params(52),
        cost_estimate=cost(1 << 20, 12 << 20),
        name="ratings",
    )(ratings)
    send_order, values = lax.optimization_barrier((send_order, values))
    split_shapes = [struct((2, n_users, rank), BF16), struct((2, rank, n_users), BF16)]
    deal, partial, meta, left, left_t = pl.pallas_call(
        before_kernel,
        out_shape=[
            struct((n_items, n_items), BF16),
            struct((n_items, rank), F32),
            struct((8, 128), F32),
        ] + split_shapes,
        in_specs=[VM, HBM, VM, HBM],
        out_specs=[VM] * 5,
        scratch_shapes=[
            pltpu.VMEM((n_items, depth), BF16),
            pltpu.VMEM((n_users, rank), F32),
            pltpu.SemaphoreType.DMA((2,)),
        ],
        compiler_params=params(),
        cost_estimate=cost(2 * n_items * n_items * depth, 6 << 20),
        name="before",
    )(send_order, item_content, projection, user_factors)
    coded = pl.pallas_call(
        project_kernel,
        out_shape=struct((n_items, rank // 2), I32),
        in_specs=[VM] * 6,
        out_specs=VM,
        compiler_params=params(),
        cost_estimate=cost(2 * n_items * n_items * depth, 4 << 20),
        name="project",
    )(deal, came[0], came[1], projection, partial, meta)
    dealt = lax.all_to_all(
        coded.reshape(n_blk, share, rank // 2), "blk", split_axis=0, concat_axis=0, tiled=True
    ).reshape(n_items, rank // 2)

    state_shapes = [struct((2, n_users, n_items), BF16), struct((2, rank, n_items), BF16)]
    ring = [(i, (i + 1) % n_blk) for i in range(n_blk)]
    pair = [(i, i ^ 1) for i in range(n_blk)]
    light = cost(1 << 10, 1 << 10)

    def push(turn, t, left, source, tail, pieces=1):
        err, right, *sent = pl.pallas_call(
            functools.partial(push_kernel, turn, t),
            out_shape=state_shapes + [struct((rank // 2 + tail, n_items // pieces), I32)] * pieces,
            in_specs=[VM] * (3 + len(source)),
            out_specs=[VM] * (2 + pieces),
            compiler_params=params(),
            cost_estimate=light,
            name="push",
        )(left, left_t, values, *source)
        return (err, right), sent

    users = user_factors
    for_odd = for_even = [dealt, meta]
    for t in range(ROUNDS - 1):
        pieces = 1 if t < ROUNDS - 2 else 2
        odd_state, sent = push(1, t, left, for_odd, EVEN_TAIL, pieces)
        next_even = [lax.ppermute(x, "blk", ring) for x in sent]
        later, _ = lax.optimization_barrier((left, sent[0]))
        even_state, sent = push(0, t, later, for_even, ODD_TAIL, pieces)
        next_odd = [lax.ppermute(x, "blk", pair) for x in sent]
        users, left, left_t = pl.pallas_call(
            pull_kernel,
            out_shape=[struct((n_users, rank), F32)] + split_shapes,
            in_specs=[VM] * 5,
            out_specs=[VM] * 3,
            compiler_params=params(),
            cost_estimate=light,
            name="pull",
        )(users, *odd_state, *even_state)
        for_even, for_odd = next_even, next_odd

    anywhere = pl.BlockSpec(memory_space=pl.ANY)
    scratch = [pltpu.VMEM((2, n_users, wide), BF16), pltpu.VMEM((2, rank, wide), BF16), pltpu.VMEM((wide, rank), F32)]
    items, part = pl.pallas_call(
        last_first_kernel,
        out_shape=[pltpu.HBM((n_items, rank), F32), struct((n_users, rank), F32)],
        in_specs=[VM] * 6,
        out_specs=[anywhere, VM],
        scratch_shapes=scratch + [pltpu.SemaphoreType.DMA((wide // CHUNK,))],
        compiler_params=params(),
        cost_estimate=light,
        name="last_first",
    )(left, left_t, values, users, for_odd[0], for_even[0])
    items, users = pl.pallas_call(
        last_second_kernel,
        out_shape=[struct((n_items, rank), F32), struct((n_users, rank), F32)],
        in_specs=[VM] * 6 + [anywhere],
        out_specs=[anywhere] * 2,
        scratch_shapes=scratch + [
            pltpu.VMEM((n_users, rank), F32),
            pltpu.SemaphoreType.DMA((wide // CHUNK + 2,)),
        ],
        input_output_aliases={6: 0},
        compiler_params=params(),
        cost_estimate=light,
        name="last_second",
    )(left, left_t, values, part, for_odd[1], for_even[1], items)
    return users, items


def solution(mesh):
    placed = (
        P("blk", "cat"),
        P(),
        P(("blk", "cat"), None),
        P(("blk", "cat"), None),
        P(("blk", "cat"), None, None),
    )
    return jax.shard_map(
        functools.partial(body, mesh.shape["blk"]),
        mesh=mesh,
        in_specs=placed,
        out_specs=(P(("blk", "cat"), None), P(("blk", "cat"), None)),
        check_vma=False,
    )
```
